512 devices in a mesh: dp: 32 (over y, x), group: 16 (over z, core).
Axes of the slice: x: 4, y: 8, z: 8, core: 2. Of those that a mesh axis runs over, the one named last changes fastest.
Arguments:
- tokens: bfloat16 [163840, 768], P(('dp', 'group')), may hold values from -6 to 6
- cotangent: bfloat16 [163840, 768], P(('dp', 'group')), may hold values from -18 to 18
- patch_mask: int32 [163840], P(('dp', 'group')), may hold values 0 or 1
- image_tiles: int32 [512, 3], replicated, may hold values from 0 to 9, as said below
- patches: int32 [512, 3], replicated, may hold values from 0 to 288, as said below
- w_in: bfloat16 [288, 384], replicated, may hold values from -0.375 to 0.375
- b_in: float32 [384], replicated, may hold values from -1 to 1
- w_out: bfloat16 [384, 288], replicated, may hold values from -0.3125 to 0.3125
- ln_gain: float32 [768], replicated, may hold values from 0.5 to 1.5
- ln_shift: float32 [768], replicated, may hold values from -0.5 to 0.5
Outputs:
- dtokens: bfloat16 [163840, 768], P(('dp', 'group'))
- grad_w_in: bfloat16 [288, 384], replicated
- grad_b_in: bfloat16 [384], replicated
- grad_w_out: bfloat16 [384, 288], replicated
- grad_b_out: bfloat16 [288], replicated
- grad_gain: bfloat16 [768], replicated
- grad_shift: bfloat16 [768], replicated
The draws below stay inside these ranges and needn't reach their ends.
Inputs may be any that keep to these rules, and one draw needn't show every extreme that they name: `image_tiles`: entry s of row d is the number of tiles of the s-th image slot of device row d, 0 for an empty slot. A device's tiles sum to at most 10, reached on some device. . An image has at most 9 tiles, reached in every draw. For an image of k tiles, patches lies between max(32, 32 * (k - 1) + 1) and 32 * k; it is 0 for an empty slot.
All inputs are finite; a program needn't handle non-finite values. No bound on the sum of `patch_mask` on one device may be relied on, other than what follows from the above.
Results may differ from the reference program's by a relative error of at most 0.0085.
Values may be sent and summed in bfloat16 or wider, within the bound.
A program may use at most 64 MiB of HBM per device.

```python
import math
import jax
import jax.numpy as jnp
from jax import lax

C = 768
H = 384
PMAX = 288
TILE = 32
TILES_DEV = 10
IMG_DEV = 3
TOK_DEV = 320
TOKENS = 163840
N_GROUP = 16
DEVICES = 512


def packing_tables(key):
    key = jax.random.fold_in(key, 4242)
    subkeys = jax.random.split(key, 6)
    groups = DEVICES // N_GROUP
    pair_count = N_GROUP // 2
    max_tiles = PMAX // TILE
    first_load = jax.random.randint(subkeys[0], (groups, pair_count), 0, TILES_DEV + 1)
    second_load = jax.random.randint(subkeys[1], (groups, pair_count), 0, TILES_DEV - first_load + 1)
    forced = jax.random.randint(subkeys[2], (), 0, groups)
    chosen_group = jnp.arange(groups)[:, None] == forced
    first_load = jnp.where(chosen_group & (jnp.arange(pair_count)[None, :] == 0), TILES_DEV, first_load)
    second_load = jnp.where(chosen_group, TILES_DEV - first_load, second_load)
    loads = jnp.stack([first_load, second_load], axis=2).reshape(groups, N_GROUP)
    scores = jax.random.randint(subkeys[3], (groups, N_GROUP), 0, 1 << 20) * N_GROUP + jnp.arange(N_GROUP)[None, :]
    shuffle = jnp.argsort(scores, axis=1)
    loads = jnp.take_along_axis(loads, shuffle, axis=1).reshape(DEVICES)
    full_device = loads == TILES_DEV
    remain = loads
    columns = []
    for slot_index in range(IMG_DEV):
        slots_left = IMG_DEV - 1 - slot_index
        low_bound = jnp.maximum(0, remain - max_tiles * slots_left)
        high_bound = jnp.minimum(max_tiles, remain)
        if slot_index == 0:
            low_bound = jnp.where(full_device, high_bound, low_bound)
        taken_tiles = jax.random.randint(jax.random.fold_in(subkeys[4], slot_index), (DEVICES,), low_bound, high_bound + 1)
        columns.append(taken_tiles)
        remain = remain - taken_tiles
    tile_table = jnp.stack(columns, axis=1).astype(jnp.int32)
    filled = tile_table > 0
    low_patch = jnp.where(filled, jnp.maximum(TILE, TILE * (tile_table - 1) + 1), 0)
    high_patch = jnp.where(filled, TILE * tile_table + 1, 1)
    counts = jax.random.randint(subkeys[5], tile_table.shape, low_patch, high_patch)
    return (tile_table, counts.astype(jnp.int32))


def draw_image_tiles(key, part):
    return packing_tables(key)[0]


def draw_patches(key, part):
    return packing_tables(key)[1]


def draw_cotangent(key, part):
    subkeys = jax.random.split(jax.random.fold_in(key, 11), 2)
    base = jnp.clip(jax.random.normal(subkeys[0], (TOKENS, C), jnp.float32), -4.0, 4.0)
    row_scale = jnp.exp(jax.random.uniform(subkeys[1], (TOKENS, 1), jnp.float32, math.log(0.3), math.log(3.0)))
    values = base * row_scale
    return values.astype(jnp.bfloat16)


def touch_ends(drawn, stream_key, smallest, top_value):
    dims = drawn.shape
    index_at = [jax.random.randint(jax.random.fold_in(stream_key, axis), (), 0, dims[axis]) for axis in range(len(dims))]
    drawn = drawn.at[tuple(index_at)].set(smallest)
    longest = dims.index(max(dims))
    index_at[longest] = (index_at[longest] + 1) % dims[longest]
    return drawn.at[tuple(index_at)].set(top_value)


def shard_levels(stream_key, shape, cuts, least, high):
    factor_of, own = 1.0, jax.random.fold_in(stream_key, 6)
    for axis_at, parts in cuts:
        draws = jnp.exp(jax.random.uniform(jax.random.fold_in(own, axis_at), (parts,), jnp.float32, least / len(cuts), high / len(cuts)))
        factor_of = factor_of * jnp.repeat(draws, shape[axis_at] // parts).reshape([-1 if axis == axis_at else 1 for axis in range(len(shape))])
    return factor_of


def scatter_about(rng, dims, scale, bound, shards=(), kind=jnp.bfloat16):
    loudness = shard_levels(rng, dims, shards, -0.22, 0.18) if shards else 1.0
    result = jax.random.normal(rng, dims, jnp.float32) * scale * loudness
    return jnp.minimum(jnp.maximum(result, -bound), bound).astype(kind)


def setup_inputs(seed: int = 0) -> dict:
    arg_keys = jax.random.split(jax.random.key(seed), 11)
    return {
        "tokens": scatter_about(arg_keys[0], (TOKENS, C), 1.0, 6.0, ((0, 512),)),
        "cotangent": draw_cotangent(jax.random.fold_in(arg_keys[10], 71), 0),
        "patch_mask": touch_ends((jax.random.randint(arg_keys[2], (TOKENS,), 0, 8) < 7).astype(jnp.int32), jax.random.fold_in(arg_keys[2], 1), 0, 1),
        "image_tiles": draw_image_tiles(jax.random.fold_in(arg_keys[10], 71), 0),
        "patches": draw_patches(jax.random.fold_in(arg_keys[10], 71), 0),
        "w_in": scatter_about(arg_keys[5], (PMAX, H), PMAX ** -0.5, 0.375),
        "b_in": jnp.clip(jax.random.uniform(arg_keys[6], (H,), jnp.float32, -1.0, 1.0), -1.0, 1.0),
        "w_out": scatter_about(arg_keys[7], (H, PMAX), H ** -0.5, 0.3125),
        "ln_gain": jnp.clip(1.0 + 0.1 * jax.random.normal(arg_keys[8], (C,), jnp.float32), 0.5, 1.5),
        "ln_shift": jnp.clip(jax.random.uniform(arg_keys[9], (C,), jnp.float32, -0.5, 0.5), -0.5, 0.5),
    }


highest = lax.Precision.HIGHEST
ln_epsilon = 1e-05
clip_share = 0.5

def gelu_pair(preact):
    normal_cdf = 0.5 * (1.0 + lax.erf(preact * 0.7071067811865476))
    density = jnp.exp(-0.5 * preact * preact) * 0.3989422804014327
    return (preact * normal_cdf, normal_cdf + preact * density)

def layout(tile_row, patch_row):
    starts = (jnp.cumsum(tile_row) - tile_row).astype(jnp.int32)
    places = jnp.arange(TILES_DEV, dtype=jnp.int32)
    inside = (places[:, None] >= starts[None, :]) & (places[:, None] < (starts + tile_row)[None, :])
    offset = places[:, None] - starts[None, :]
    row_place = offset[:, :, None] * TILE + jnp.arange(TILE, dtype=jnp.int32)[None, None, :]
    alive = lax.optimization_barrier(jnp.sum((inside[:, :, None] & (row_place < patch_row[None, :, None])).astype(jnp.int32), axis=1))
    return (inside, offset, alive)

def device_terms(tok_block, cot_block, mask_block, tile_row, patch_row, w_in, b_in, w_out, ln_gain, ln_shift):
    spans = PMAX // TILE
    inside, offset, alive = layout(tile_row, patch_row)
    alive_rows = (alive.reshape(-1) * mask_block).astype(jnp.float32)
    values = tok_block.astype(jnp.float32)
    center = values - lax.optimization_barrier(jnp.mean(values, axis=1, keepdims=True))
    inv_std = lax.rsqrt(lax.optimization_barrier(jnp.mean(center * center, axis=1, keepdims=True)) + ln_epsilon)
    normal_x = center * inv_std
    normed = ((normal_x * ln_gain + ln_shift) * alive_rows[:, None]).astype(jnp.bfloat16)
    dout = (cot_block.astype(jnp.float32) * alive_rows[:, None]).astype(jnp.bfloat16)
    img_hot = inside.astype(jnp.float32)
    tile_alive = lax.optimization_barrier(jnp.sum(inside.astype(jnp.int32), axis=1))
    span_index = lax.optimization_barrier(jnp.sum(jnp.where(inside, offset, 0), axis=1)).astype(jnp.int32)
    span_hot = ((span_index[:, None] == jnp.arange(spans, dtype=jnp.int32)[None, :]) & (tile_alive[:, None] > 0)).astype(jnp.float32)
    image_index = lax.optimization_barrier(jnp.sum(jnp.where(inside, jnp.arange(IMG_DEV, dtype=jnp.int32)[None, :], 0), axis=1)).astype(jnp.int32)
    alive_tile = tile_alive.astype(jnp.float32)
    rows_in = jnp.take(w_in.reshape(spans, TILE, H).astype(jnp.float32), span_index, axis=0) * alive_tile[:, None, None]
    cols_out = jnp.transpose(jnp.take(w_out.reshape(H, spans, TILE).astype(jnp.float32), span_index, axis=1), (1, 0, 2)) * alive_tile[:, None, None]
    y_tiles = normed.astype(jnp.float32).reshape(TILES_DEV, TILE, C)
    o_tiles = dout.astype(jnp.float32).reshape(TILES_DEV, TILE, C)
    part_pre = jnp.einsum('tpc,tph->tch', y_tiles, rows_in, precision=highest)
    part_dz = jnp.einsum('tpc,thp->tch', o_tiles, cols_out, precision=highest)
    preact = jnp.einsum('ts,tch->sch', img_hot, part_pre, precision=highest) + b_in
    dz_all = jnp.einsum('ts,tch->sch', img_hot, part_dz, precision=highest)
    act, slope = gelu_pair(preact)
    act_b = act.astype(jnp.bfloat16)
    dpre = dz_all * slope
    dpre_b = dpre.astype(jnp.bfloat16)
    grad_b_in = lax.optimization_barrier(jnp.sum(dpre, axis=(0, 1)))
    z_tiles = jnp.take(act_b.astype(jnp.float32), image_index, axis=0)
    da_tiles = jnp.take(dpre_b.astype(jnp.float32), image_index, axis=0)
    grad_in_tiles = jnp.einsum('tpc,tch->tph', y_tiles, da_tiles, precision=highest)
    grad_w_in = jnp.einsum('tj,tph->jph', span_hot, grad_in_tiles, precision=highest).reshape(PMAX, H)
    grad_out_tiles = jnp.einsum('tch,tpc->thp', z_tiles, o_tiles, precision=highest)
    grad_w_out = jnp.einsum('tj,thp->hjp', span_hot, grad_out_tiles, precision=highest).reshape(H, PMAX)
    grad_b_out = jnp.einsum('tj,tp->jp', span_hot, lax.optimization_barrier(jnp.sum(o_tiles, axis=2)), precision=highest).reshape(PMAX)
    dnormed = jnp.einsum('tch,tph->tpc', da_tiles, rows_in, precision=highest).astype(jnp.bfloat16).reshape(TOK_DEV, C)
    d_rows = dnormed.astype(jnp.float32) * alive_rows[:, None]
    grad_gain = lax.optimization_barrier(jnp.sum(d_rows * normal_x, axis=0))
    grad_shift = lax.optimization_barrier(jnp.sum(d_rows, axis=0))
    scaled = d_rows * ln_gain
    inner = lax.optimization_barrier(jnp.mean(scaled * normal_x, axis=1, keepdims=True))
    d_norm = (scaled - lax.optimization_barrier(jnp.mean(scaled, axis=1, keepdims=True)) - normal_x * inner) * inv_std
    dtok = (cot_block.astype(jnp.float32) + d_norm).astype(jnp.bfloat16)
    return ((grad_w_in, grad_b_in, grad_w_out, grad_b_out, grad_gain, grad_shift), dtok)

def reference(tokens, cotangent, patch_mask, image_tiles, patches, w_in, b_in, w_out, ln_gain, ln_shift):
    tok_all = tokens.reshape(DEVICES, TOK_DEV, C)
    cot_all = cotangent.reshape(DEVICES, TOK_DEV, C)
    mask_all = patch_mask.reshape(DEVICES, TOK_DEV)
    start_sums = (jnp.zeros((PMAX, H), jnp.float32), jnp.zeros((H,), jnp.float32), jnp.zeros((H, PMAX), jnp.float32), jnp.zeros((PMAX,), jnp.float32), jnp.zeros((C,), jnp.float32), jnp.zeros((C,), jnp.float32))

    def visit(totals, blocks):
        terms, dtok = device_terms(blocks[0], blocks[1], blocks[2], blocks[3], blocks[4], w_in, b_in, w_out, ln_gain, ln_shift)
        return (tuple((left + right for left, right in zip(totals, terms))), dtok)
    totals, dtoks = lax.scan(visit, start_sums, (tok_all, cot_all, mask_all, image_tiles, patches))
    total = sum((jnp.sum(piece * piece) for piece in totals))
    entries = 2 * PMAX * H + H + PMAX + 2 * C
    factor = jnp.minimum(1.0, clip_share * math.sqrt(entries) / jnp.sqrt(total + 1e-06))
    clipped = tuple(((piece * factor).astype(jnp.bfloat16) for piece in totals))
    return (dtoks.reshape(TOKENS, C), clipped[0], clipped[1], clipped[2], clipped[3], clipped[4], clipped[5])
```

```python
import math

import jax
import jax.numpy as jnp
from jax import lax
from jax.experimental import pallas as pl
from jax.experimental.pallas import tpu as pltpu
from jax.sharding import PartitionSpec as P

PMAX = 288
TILE = 32
TILES = 10
ROWS = TILE * TILES
C = 768
H = 384
NX = 4
SPANS = (288, 160, 96)
BASES = (0, 288, 448)
PAD_ROWS = ROWS + PMAX
LINES = 16
BLOCKS = 64
ENTRIES = 2 * PMAX * H + H + PMAX + 2 * C

ln_epsilon = 1e-05
clip_share = 0.5
F32 = jnp.float32
BF16 = jnp.bfloat16
MESH = pl.DeviceIdType.MESH
AXES = ("dp", "group")
VMEM = pl.BlockSpec(memory_space=pltpu.VMEM)
SMEM = pl.BlockSpec(memory_space=pltpu.SMEM)


def dot(a, b, da, db):
    return lax.dot_general(a, b, (((da,), (db,)), ((), ())), preferred_element_type=F32)


def gelu_pair(preact):
    normal_cdf = 0.5 * (1.0 + lax.erf(preact * 0.7071067811865476))
    density = jnp.exp(-0.5 * preact * preact) * 0.3989422804014327
    return (preact * normal_cdf, normal_cdf + preact * density)


def wide(col):
    return jnp.concatenate([col] * (C // 128), axis=1)


def column(row):
    return jnp.transpose(jnp.broadcast_to(row, (128, row.shape[1])))


def image_table(tiles_ref, patches_ref, place):
    tiles = [tiles_ref[s, place] for s in range(3)]
    counts = [patches_ref[s, place] for s in range(3)]
    starts = [jnp.int32(0), tiles[0], tiles[0] + tiles[1]]
    images = list(zip(tiles, starts, counts))
    for i, j in ((0, 1), (0, 2), (1, 2)):
        a, b = images[i], images[j]
        swap = b[0] > a[0]
        images[i] = tuple(jnp.where(swap, q, p) for p, q in zip(a, b))
        images[j] = tuple(jnp.where(swap, p, q) for p, q in zip(a, b))
    return images


def compute_kernel(
    tiles_ref, patches_ref, tok_ref, cot_ref, mask_ref, wi_ref, bi_ref, wo_ref, gain_ref, shift_ref,
    dtok_ref, pack_ref,
    nx_ref, inv_ref, alive_ref, x_ref, d_ref, dn_ref, act_ref, dpre_ref, gi_ref, go_ref, bo_ref, small_ref,
):
    place = lax.axis_index("dp") * lax.axis_size("group") + lax.axis_index("group")
    images = image_table(tiles_ref, patches_ref, place)
    row = lax.broadcasted_iota(jnp.int32, (ROWS, 128), 0)
    alive = jnp.zeros((ROWS, 128), F32)
    for _, start, count in images:
        first = start * TILE
        alive = jnp.where((row >= first) & (row < first + count), 1.0, alive)
    alive_ref[...] = alive * column(mask_ref[...].astype(F32))
    gain = gain_ref[...]
    shift = shift_ref[...]
    x_ref[ROWS:, :] = jnp.zeros((PMAX, C), BF16)
    d_ref[ROWS:, :] = jnp.zeros((PMAX, C), BF16)
    for t in range(TILES):
        rows = slice(t * TILE, (t + 1) * TILE)
        live = wide(alive_ref[rows, :])
        values = tok_ref[rows, :].astype(F32)
        center = values - jnp.mean(values, axis=1, keepdims=True)
        inv = lax.rsqrt(jnp.mean(center * center, axis=1, keepdims=True) + ln_epsilon)
        normal = center * inv
        nx_ref[rows, :] = normal
        inv_ref[rows, :] = jnp.broadcast_to(inv, (TILE, 128))
        x_ref[rows, :] = ((normal * gain + shift) * live).astype(BF16)
        d_ref[rows, :] = (cot_ref[rows, :].astype(F32) * live).astype(BF16)

    bias = column(bi_ref[...])
    ones = jnp.ones((16, C), BF16)
    bo_ref[...] = jnp.zeros((16, H), F32)
    sums = [jnp.zeros((128, 128), F32) for _ in range(3)]
    for j, (tiles, start, _) in enumerate(images):
        span = SPANS[j]
        first = pl.multiple_of(start * TILE, TILE)
        inside = lax.broadcasted_iota(jnp.int32, (span, 128), 0) < tiles * TILE
        inside = wide(inside.astype(F32).astype(BF16))
        xs = x_ref[pl.ds(first, span), :] * inside
        ds = d_ref[pl.ds(first, span), :] * inside
        for h in range(3):
            lines = slice(h * 128, (h + 1) * 128)
            preact = dot(wi_ref[:span, lines], xs, 0, 0) + wide(bias[lines, :])
            dz = dot(wo_ref[:span, lines], ds, 0, 0)
            act, slope = gelu_pair(preact)
            act_ref[lines, :] = act.astype(BF16)
            dpre = dz * slope
            dpre_ref[lines, :] = dpre.astype(BF16)
            for b in range(C // 128):
                sums[h] = sums[h] + dpre[:, b * 128 : (b + 1) * 128]
        gi = dot(xs, dpre_ref[...], 1, 1)
        go = dot(ds, act_ref[...], 1, 1)
        bo = dot(ones, ds, 1, 1)
        if j == 0:
            gi_ref[...] = gi
            go_ref[...] = go
            bo_ref[:, :span] = bo
        else:
            gi_ref[:span, :] += gi
            go_ref[:span, :] += go
            bo_ref[:, :span] += bo
        dn_ref[BASES[j] : BASES[j] + span, :] = dot(wi_ref[:span, :], dpre_ref[...], 1, 0).astype(BF16)

    gain_sum = jnp.zeros((8, C), F32)
    shift_sum = jnp.zeros((8, C), F32)
    for t in range(TILES):
        rows = slice(t * TILE, (t + 1) * TILE)
        source = jnp.int32(0)
        for j, (tiles, start, _) in enumerate(images):
            held = (start <= t) & (t < start + tiles)
            source = jnp.where(held, BASES[j] + (t - start) * TILE, source)
        source = pl.multiple_of(source, TILE)
        normal = nx_ref[rows, :]
        d_rows = dn_ref[pl.ds(source, TILE), :].astype(F32) * wide(alive_ref[rows, :])
        weighted = d_rows * normal
        for i in range(0, TILE, 8):
            gain_sum = gain_sum + weighted[i : i + 8]
            shift_sum = shift_sum + d_rows[i : i + 8]
        scaled = d_rows * gain
        inner = jnp.mean(scaled * normal, axis=1, keepdims=True)
        d_norm = (scaled - jnp.mean(scaled, axis=1, keepdims=True) - normal * inner) * wide(inv_ref[rows, :])
        dtok_ref[rows, :] = (cot_ref[rows, :].astype(F32) + d_norm).astype(BF16)

    small_ref[...] = jnp.zeros((2 * LINES, 128), F32)
    gain_row = jnp.sum(gain_sum, axis=0, keepdims=True)
    shift_row = jnp.sum(shift_sum, axis=0, keepdims=True)
    for b in range(6):
        small_ref[b : b + 1, :] = gain_row[:, b * 128 : (b + 1) * 128]
        small_ref[6 + b : 7 + b, :] = shift_row[:, b * 128 : (b + 1) * 128]
    for b in range(3):
        small_ref[16 + b : 17 + b, :] = jnp.sum(jnp.transpose(sums[b]), axis=0, keepdims=True)
        small_ref[19 + b : 20 + b, :] = bo_ref[0:1, b * 128 : (b + 1) * 128]
    for i in range(PMAX // LINES):
        for b in range(3):
            box = (slice(i * LINES, (i + 1) * LINES), slice(b * 128, (b + 1) * 128))
            pack_ref[0, i * 3 + b] = gi_ref[box].astype(BF16)
            pack_ref[1, i * 3 + b] = go_ref[box].astype(BF16)
    pack_ref[0, 54] = small_ref[:LINES, :].astype(BF16)
    pack_ref[0, 55] = small_ref[LINES:, :].astype(BF16)
    pack_ref[0, 56:] = jnp.zeros((8, LINES, 128), BF16)
    pack_ref[1, 54:] = jnp.zeros((10, LINES, 128), BF16)


def ring_order(n):
    order = []
    for d in range(1, n // 2 + 1):
        order.append(d)
        if n - d != d:
            order.append(n - d)
    return order


def copy_to(source, target, sems, device):
    send, recv = sems
    copy = pltpu.make_async_remote_copy(
        src_ref=source, dst_ref=target, send_sem=send, recv_sem=recv, device_id=device, device_id_type=MESH
    )
    copy.start()
    return copy


def comm_kernel(
    nx, ny, nz,
    pack_ref, out_ref,
    r0, q, r1, t_ref, r2, u_ref, r3,
    s0, v0, s1, v1, s2, v2, s3, v3, s4, v4, s5, v5, s6, v6,
):
    dp = lax.axis_index("dp")
    group = lax.axis_index("group")
    y, x = dp // nx, lax.rem(dp, nx)
    z, c = group // 2, lax.rem(group, 2)
    mate = 1 - c
    chip = (nz, ny)
    mine = (z, y)
    partner = (dp, z * 2 + mate)

    def z_peer(d):
        return (dp, lax.rem(z + d, nz) * 2 + c)

    def y_peer(d):
        return (lax.rem(y + d, ny) * nx + x, group)

    def x_peer(d):
        return (y * nx + lax.rem(x + d, nx), group)

    peers = (z_peer, y_peer)
    barrier = pltpu.get_barrier_semaphore()
    everyone = [partner]
    everyone += [z_peer(d) for d in range(1, nz)]
    everyone += [y_peer(d) for d in range(1, ny)]
    everyone += [x_peer(d) for d in range(1, nx)]
    for device in everyone:
        pl.semaphore_signal(barrier, inc=1, device_id=device, device_id_type=MESH)
    pl.semaphore_wait(barrier, len(everyone))
    copies = []

    first = {}
    orders = [list(reversed(ring_order(n))) + [0] for n in chip]
    for step in range(max(chip)):
        for k in (0, 1):
            if step < chip[k]:
                d = orders[k][step]
                at = lax.rem(mine[k] + d, chip[k])
                first[k, d] = copy_to(
                    pack_ref.at[k, mate, at], r0.at[k, at], (s0.at[k, d], v0.at[k, d]), partner
                )
                copies.append(first[k, d])
    second = {}
    for step in range(max(chip)):
        for k in (0, 1):
            if step < chip[k]:
                d = orders[k][step]
                at = lax.rem(mine[k] + d, chip[k])
                first[k, d].wait_recv()
                q[k, at] = (pack_ref[k, c, at].astype(F32) + r0[k, at].astype(F32)).astype(BF16)
                if d:
                    second[k, d] = copy_to(
                        q.at[k, at], r1.at[k, mine[k]], (s1.at[k, d], v1.at[k, d]), peers[k](d)
                    )
                    copies.append(second[k, d])
    for k in (0, 1):
        total = q[k, mine[k]].astype(F32)
        for d in ring_order(chip[k]):
            second[k, d].wait_recv()
            total = total + r1[k, lax.rem(mine[k] - d + chip[k], chip[k])].astype(F32)
        t_ref[:, k] = total.astype(BF16)
    third = {}
    for d in reversed(ring_order(nx)):
        third[d] = copy_to(t_ref.at[lax.rem(x + d, nx)], r2.at[x], (s2.at[d], v2.at[d]), x_peer(d))
        copies.append(third[d])
    total = t_ref[x].astype(F32)
    for d in ring_order(nx):
        third[d].wait_recv()
        total = total + r2[lax.rem(x - d + nx, nx)].astype(F32)
    u_ref[...] = total.astype(BF16)
    fourth = {}
    for k in (0, 1):
        n = chip[1 - k]
        for d in reversed(ring_order(n)):
            fourth[k, d] = copy_to(
                u_ref.at[k], r3.at[k, mine[1 - k]], (s3.at[k, d], v3.at[k, d]), peers[1 - k](d)
            )
            copies.append(fourth[k, d])
        r3[k, mine[1 - k]] = u_ref[k]
    fifth = {}
    for k in (0, 1):
        n = chip[1 - k]
        for d in ring_order(n):
            fourth[k, d].wait_recv()
        total = r3[k, 0].astype(F32)
        for i in range(1, n):
            total = total + r3[k, i].astype(F32)
        out_ref[k, c, mine[k], x] = total.astype(BF16)
        block = out_ref.at[k, c, mine[k], x]
        for d in reversed(ring_order(nx)):
            fifth[k, d] = copy_to(block, block, (s4.at[k, d], v4.at[k, d]), x_peer(d))
            copies.append(fifth[k, d])
    sixth = {}
    last = {}
    for k in (0, 1):
        for d in ring_order(nx):
            fifth[k, d].wait_recv()
        block = out_ref.at[k, c, mine[k]]
        for d in reversed(ring_order(chip[k])):
            sixth[k, d] = copy_to(block, block, (s5.at[k, d], v5.at[k, d]), peers[k](d))
            copies.append(sixth[k, d])
        last[k, 0] = copy_to(block, block, (s6.at[k, 0], v6.at[k, 0]), partner)
        copies.append(last[k, 0])
    orders = [ring_order(n) for n in chip]
    for step in range(max(chip) - 1):
        for k in (0, 1):
            if step < chip[k] - 1:
                d = orders[k][step]
                sixth[k, d].wait_recv()
                block = out_ref.at[k, c, lax.rem(mine[k] - d + chip[k], chip[k])]
                last[k, d] = copy_to(block, block, (s6.at[k, d], v6.at[k, d]), partner)
                copies.append(last[k, d])
    for copy in last.values():
        copy.wait_recv()
    for copy in copies:
        copy.wait_send()


def finish_kernel(sum_ref, wi_ref, bi_ref, wo_ref, bo_ref, gain_ref, shift_ref):
    total = jnp.zeros((LINES, 128), F32)
    for k in (0, 1):
        for i in range(56 - 2 * k):
            piece = sum_ref[k, i].astype(F32)
            total = total + piece * piece
    total = jnp.sum(jnp.sum(total, axis=1, keepdims=True), axis=0, keepdims=True)
    factor = jnp.minimum(1.0, clip_share * math.sqrt(ENTRIES) / jnp.sqrt(total + 1e-06))
    for i in range(PMAX // LINES):
        for b in range(3):
            box = (slice(i * LINES, (i + 1) * LINES), slice(b * 128, (b + 1) * 128))
            wi_ref[box] = (sum_ref[0, i * 3 + b].astype(F32) * factor).astype(BF16)
            wo_ref[box] = (sum_ref[1, i * 3 + b].astype(F32) * factor).astype(BF16)
    one = sum_ref[0, 54].astype(F32) * factor
    two = sum_ref[0, 55].astype(F32) * factor
    for b in range(6):
        at = slice(b * 128, (b + 1) * 128)
        gain_ref[:, at] = one[b : b + 1].astype(BF16)
        shift_ref[:, at] = one[6 + b : 7 + b].astype(BF16)
    for b in range(3):
        at = slice(b * 128, (b + 1) * 128)
        bi_ref[:, at] = two[b : b + 1].astype(BF16)
        bo_ref[:, at] = two[3 + b : 4 + b].astype(BF16)


def compute(tokens, cotangent, patch_mask, image_tiles, patches, w_in, b_in, w_out, ln_gain, ln_shift):
    shape = jax.ShapeDtypeStruct
    return pl.pallas_call(
        compute_kernel,
        name="compute",
        out_shape=(shape((ROWS, C), BF16), shape((2, BLOCKS, LINES, 128), BF16)),
        in_specs=[SMEM, SMEM] + [VMEM] * 8,
        out_specs=(VMEM, VMEM),
        scratch_shapes=[
            pltpu.VMEM((ROWS, C), F32),
            pltpu.VMEM((ROWS, 128), F32),
            pltpu.VMEM((ROWS, 128), F32),
            pltpu.VMEM((PAD_ROWS, C), BF16),
            pltpu.VMEM((PAD_ROWS, C), BF16),
            pltpu.VMEM((sum(SPANS), C), BF16),
            pltpu.VMEM((H, C), BF16),
            pltpu.VMEM((H, C), BF16),
            pltpu.VMEM((PMAX, H), F32),
            pltpu.VMEM((PMAX, H), F32),
            pltpu.VMEM((16, H), F32),
            pltpu.VMEM((2 * LINES, 128), F32),
        ],
    )(
        image_tiles.T, patches.T, tokens, cotangent, patch_mask.reshape(1, ROWS), w_in,
        b_in.reshape(1, H), w_out.T, ln_gain.reshape(1, C), ln_shift.reshape(1, C),
    )


def total_of(packed, nx, ny, nz):
    n = max(ny, nz)
    dma = pltpu.SemaphoreType.DMA
    block = (LINES, 128)
    sems = [(2, n), (2, n), (nx,), (2, n), (2, nx), (2, n), (2, n)]
    return pl.pallas_call(
        lambda *refs: comm_kernel(nx, ny, nz, *refs),
        name="exchange",
        out_shape=jax.ShapeDtypeStruct((2, 2, n, nx, *block), BF16),
        in_specs=[VMEM],
        out_specs=VMEM,
        scratch_shapes=[
            pltpu.VMEM((2, n, nx, *block), BF16),
            pltpu.VMEM((2, n, nx, *block), BF16),
            pltpu.VMEM((2, n, nx, *block), BF16),
            pltpu.VMEM((nx, 2, *block), BF16),
            pltpu.VMEM((nx, 2, *block), BF16),
            pltpu.VMEM((2, *block), BF16),
            pltpu.VMEM((2, n, *block), BF16),
        ]
        + [dma(shape) for shape in sems for _ in range(2)],
        compiler_params=pltpu.CompilerParams(collective_id=0, has_side_effects=True),
    )(packed.reshape(2, 2, n, nx, *block))


def finish(sums):
    shape = jax.ShapeDtypeStruct
    shapes = ((PMAX, H), (1, H), (PMAX, H), (1, H), (1, C), (1, C))
    return pl.pallas_call(
        finish_kernel,
        name="finish",
        out_shape=tuple(shape(s, BF16) for s in shapes),
        in_specs=[VMEM],
        out_specs=(VMEM,) * 6,
    )(sums)


def solution(mesh):
    ny, nz = mesh.shape["dp"] // NX, mesh.shape["group"] // 2

    def local(*args):
        dtokens, packed = compute(*args)
        sums = total_of(packed, NX, ny, nz).reshape(2, BLOCKS, LINES, 128)
        w_in, b_in, w_out, b_out, gain, shift = finish(sums)
        return (
            dtokens, w_in, b_in.reshape(H), w_out.T, b_out.reshape(H)[:PMAX], gain.reshape(C), shift.reshape(C)
        )

    rows = P(AXES, None)
    in_specs = (rows, rows, P(AXES)) + (P(),) * 7
    out_specs = (rows,) + (P(),) * 6
    return jax.shard_map(local, mesh=mesh, in_specs=in_specs, out_specs=out_specs, check_vma=False)
```

```python
import math

import jax
import jax.numpy as jnp
from jax import lax
from jax.experimental import pallas as pl
from jax.experimental.pallas import tpu as pltpu
from jax.sharding import PartitionSpec as P

PMAX = 288
TILE = 32
TILES = 10
ROWS = TILE * TILES
C = 768
H = 384
NX = 4
SPANS = (288, 160, 96)
BASES = (0, 9, 14)
PAD_TILES = TILES + PMAX // TILE
LINES = 16
BLOCKS = 64
ENTRIES = 2 * PMAX * H + H + PMAX + 2 * C

ln_epsilon = 1e-05
clip_share = 0.5
F32 = jnp.float32
BF16 = jnp.bfloat16
MESH = pl.DeviceIdType.MESH
AXES = ("dp", "group")
VMEM = pl.BlockSpec(memory_space=pltpu.VMEM)
HBM = pl.BlockSpec(memory_space=pltpu.HBM)


def dot(a, b, da, db):
    return lax.dot_general(a, b, (((da,), (db,)), ((), ())), preferred_element_type=F32)


def gelu_pair(preact):
    normal_cdf = 0.5 * (1.0 + lax.erf(preact * 0.7071067811865476))
    density = jnp.exp(-0.5 * preact * preact) * 0.3989422804014327
    return (preact * normal_cdf, normal_cdf + preact * density)


def wide(col):
    return jnp.concatenate([col] * (C // 128), axis=1)


def column(row):
    return jnp.transpose(jnp.broadcast_to(row, (128, row.shape[1])))


def image_table(tiles_ref, patches_ref, place):
    tiles = [tiles_ref[s, place] for s in range(3)]
    counts = [patches_ref[s, place] for s in range(3)]
    starts = [jnp.int32(0), tiles[0], tiles[0] + tiles[1]]
    images = list(zip(tiles, starts, counts))
    for i, j in ((0, 1), (0, 2), (1, 2)):
        a, b = images[i], images[j]
        swap = b[0] > a[0]
        images[i] = tuple(jnp.where(swap, q, p) for p, q in zip(a, b))
        images[j] = tuple(jnp.where(swap, p, q) for p, q in zip(a, b))
    return images


def rows_of(images, t, dn_ref, alive_ref):
    source = jnp.int32(0)
    for j, (tiles, start, _) in enumerate(images):
        held = (start <= t) & (t < start + tiles)
        source = jnp.where(held, BASES[j] + t - start, source)
    return dn_ref[source].astype(F32) * wide(alive_ref[t * TILE : (t + 1) * TILE, :])


def gradients(
    tiles_ref, patches_ref, tok_ref, cot_ref, mask_ref, wi_ref, bi_ref, wo_ref, gain_ref, shift_ref, pack_ref,
    nx_ref, inv_ref, alive_ref, x_ref, d_ref, dn_ref, act_ref, dpre_ref, gi_ref, go_ref, bo_ref, small_ref,
):
    place = lax.axis_index("dp") * lax.axis_size("group") + lax.axis_index("group")
    images = image_table(tiles_ref, patches_ref, place)
    row = lax.broadcasted_iota(jnp.int32, (ROWS, 128), 0)
    alive = jnp.zeros((ROWS, 128), F32)
    for _, start, count in images:
        first = start * TILE
        alive = jnp.where((row >= first) & (row < first + count), 1.0, alive)
    alive_ref[...] = alive * column(mask_ref[...].astype(F32).reshape(1, ROWS))
    gain = gain_ref[...].reshape(1, C)
    shift = shift_ref[...].reshape(1, C)
    x_ref[TILES:] = jnp.zeros((PMAX // TILE, TILE, C), BF16)
    d_ref[TILES:] = jnp.zeros((PMAX // TILE, TILE, C), BF16)
    for t in range(TILES):
        rows = slice(t * TILE, (t + 1) * TILE)
        live = wide(alive_ref[rows, :])
        values = tok_ref[rows, :].astype(F32)
        center = values - jnp.mean(values, axis=1, keepdims=True)
        inv = lax.rsqrt(jnp.mean(center * center, axis=1, keepdims=True) + ln_epsilon)
        normal = center * inv
        nx_ref[rows, :] = normal
        inv_ref[rows, :] = jnp.broadcast_to(inv, (TILE, 128))
        x_ref[t] = ((normal * gain + shift) * live).astype(BF16)
        d_ref[t] = (cot_ref[rows, :].astype(F32) * live).astype(BF16)

    bias = column(bi_ref[...].reshape(1, H))
    ones = jnp.ones((16, C), BF16)
    bo_ref[...] = jnp.zeros((16, H), F32)
    sums = [jnp.zeros((128, 128), F32) for _ in range(3)]
    for j, (tiles, start, _) in enumerate(images):
        span = SPANS[j]
        steps = range(span // TILE)
        inside = lax.broadcasted_iota(jnp.int32, (span, 128), 0) < tiles * TILE
        inside = wide(inside.astype(F32).astype(BF16))
        xs = jnp.concatenate([x_ref[start + u] for u in steps]) * inside
        ds = jnp.concatenate([d_ref[start + u] for u in steps]) * inside
        for h in range(3):
            lines = slice(h * 128, (h + 1) * 128)
            preact = dot(wi_ref[:span, lines], xs, 0, 0) + wide(bias[lines, :])
            dz = dot(wo_ref[:span, lines], ds, 0, 0)
            act, slope = gelu_pair(preact)
            act_ref[lines, :] = act.astype(BF16)
            dpre = dz * slope
            dpre_ref[lines, :] = dpre.astype(BF16)
            for b in range(C // 128):
                sums[h] = sums[h] + dpre[:, b * 128 : (b + 1) * 128]
        gi = dot(xs, dpre_ref[...], 1, 1)
        go = dot(ds, act_ref[...], 1, 1)
        bo = dot(ones, ds, 1, 1)
        if j == 0:
            gi_ref[...] = gi
            go_ref[...] = go
            bo_ref[:, :span] = bo
        else:
            gi_ref[:span, :] += gi
            go_ref[:span, :] += go
            bo_ref[:, :span] += bo
        back = dot(wi_ref[:span, :], dpre_ref[...], 1, 0).astype(BF16)
        for u in steps:
            dn_ref[BASES[j] + u] = back[u * TILE : (u + 1) * TILE]

    gain_sum = jnp.zeros((8, C), F32)
    shift_sum = jnp.zeros((8, C), F32)
    for t in range(TILES):
        d_rows = rows_of(images, t, dn_ref, alive_ref)
        weighted = d_rows * nx_ref[t * TILE : (t + 1) * TILE, :]
        for i in range(0, TILE, 8):
            gain_sum = gain_sum + weighted[i : i + 8]
            shift_sum = shift_sum + d_rows[i : i + 8]

    small_ref[...] = jnp.zeros((2 * LINES, 128), F32)
    gain_row = jnp.sum(gain_sum, axis=0, keepdims=True)
    shift_row = jnp.sum(shift_sum, axis=0, keepdims=True)
    for b in range(6):
        small_ref[b : b + 1, :] = gain_row[:, b * 128 : (b + 1) * 128]
        small_ref[6 + b : 7 + b, :] = shift_row[:, b * 128 : (b + 1) * 128]
    for b in range(3):
        small_ref[16 + b : 17 + b, :] = jnp.sum(jnp.transpose(sums[b]), axis=0, keepdims=True)
        small_ref[19 + b : 20 + b, :] = bo_ref[0:1, b * 128 : (b + 1) * 128]
    n, nx, lines = pack_ref.shape[2:5]
    each = lines // LINES

    def put(k, i, value):
        shard, at = i // each, i % each * LINES
        pack_ref[k, shard // (n * nx), shard // nx % n, shard % nx, at : at + LINES] = value

    for i in range(PMAX // LINES):
        for b in range(3):
            box = (slice(i * LINES, (i + 1) * LINES), slice(b * 128, (b + 1) * 128))
            put(0, i * 3 + b, gi_ref[box].astype(BF16))
            put(1, i * 3 + b, go_ref[box].astype(BF16))
    put(0, 54, small_ref[:LINES, :].astype(BF16))
    put(0, 55, small_ref[LINES:, :].astype(BF16))
    for k, used in ((0, 56), (1, 54)):
        for i in range(used, BLOCKS):
            put(k, i, jnp.zeros((LINES, 128), BF16))
    return images


def token_gradient(images, cot_ref, gain_ref, dtok_ref, nx_ref, inv_ref, alive_ref, dn_ref):
    gain = gain_ref[...].reshape(1, C)
    for t in range(TILES):
        rows = slice(t * TILE, (t + 1) * TILE)
        normal = nx_ref[rows, :]
        scaled = rows_of(images, t, dn_ref, alive_ref) * gain
        inner = jnp.mean(scaled * normal, axis=1, keepdims=True)
        d_norm = (scaled - jnp.mean(scaled, axis=1, keepdims=True) - normal * inner) * wide(inv_ref[rows, :])
        dtok_ref[rows, :] = (cot_ref[rows, :].astype(F32) + d_norm).astype(BF16)


def ring_order(n):
    order = []
    for d in range(1, n // 2 + 1):
        order.append(d)
        if n - d != d:
            order.append(n - d)
    return order


def copy_to(source, target, sems, device):
    send, recv = sems
    copy = pltpu.make_async_remote_copy(
        src_ref=source, dst_ref=target, send_sem=send, recv_sem=recv, device_id=device, device_id_type=MESH
    )
    copy.start()
    return copy


def main_kernel(
    nx, ny, nz,
    tiles_in, patches_in, tok_in, cot_in, mask_in, wi_in, bi_in, wo_in, gain_in, shift_in,
    dtok_ref, out_ref,
    tiles_ref, patches_ref, tok_ref, cot_ref, mask_ref, wi_ref, bi_ref, wo_ref, gain_ref, shift_ref, in_sem,
    nx_ref, inv_ref, alive_ref, x_ref, d_ref, dn_ref, act_ref, dpre_ref, gi_ref, go_ref, bo_ref, small_ref,
    pack_ref, r0, q, r1, t_ref, r2, u_ref, r3,
    s0, v0, s1, v1, s2, v2, s3, v3, s4, v4, s5, v5, s6, v6,
):
    pairs = (
        (tok_in, tok_ref), (mask_in, mask_ref), (gain_in, gain_ref), (shift_in, shift_ref), (tiles_in, tiles_ref),
        (patches_in, patches_ref), (cot_in, cot_ref), (wi_in, wi_ref), (wo_in, wo_ref), (bi_in, bi_ref),
    )
    loads = [pltpu.make_async_copy(a, b, in_sem.at[i]) for i, (a, b) in enumerate(pairs)]
    for load in loads:
        load.start()
    dp = lax.axis_index("dp")
    group = lax.axis_index("group")
    y, x = dp // nx, lax.rem(dp, nx)
    z, c = group // 2, lax.rem(group, 2)
    mate = 1 - c
    chip = (nz, ny)
    mine = (z, y)
    partner = (dp, z * 2 + mate)

    def z_peer(d):
        return (dp, lax.rem(z + d, nz) * 2 + c)

    def y_peer(d):
        return (lax.rem(y + d, ny) * nx + x, group)

    def x_peer(d):
        return (y * nx + lax.rem(x + d, nx), group)

    peers = (z_peer, y_peer)
    barrier = pltpu.get_barrier_semaphore()
    everyone = [partner]
    everyone += [z_peer(d) for d in range(1, nz)]
    everyone += [y_peer(d) for d in range(1, ny)]
    everyone += [x_peer(d) for d in range(1, nx)]
    for device in everyone:
        pl.semaphore_signal(barrier, inc=1, device_id=device, device_id_type=MESH)
    for load in loads:
        load.wait()
    images = gradients(
        tiles_ref, patches_ref, tok_ref, cot_ref, mask_ref, wi_ref, bi_ref, wo_ref, gain_ref, shift_ref, pack_ref,
        nx_ref, inv_ref, alive_ref, x_ref, d_ref, dn_ref, act_ref, dpre_ref, gi_ref, go_ref, bo_ref, small_ref,
    )
    pl.semaphore_wait(barrier, len(everyone))
    copies = []

    first = {}
    orders = [list(reversed(ring_order(n))) + [0] for n in chip]
    for step in range(max(chip)):
        for k in (0, 1):
            if step < chip[k]:
                d = orders[k][step]
                at = lax.rem(mine[k] + d, chip[k])
                first[k, d] = copy_to(
                    pack_ref.at[k, mate, at], r0.at[k, at], (s0.at[k, d], v0.at[k, d]), partner
                )
                copies.append(first[k, d])
    second = {}
    for step in range(max(chip)):
        for k in (0, 1):
            if step < chip[k]:
                d = orders[k][step]
                at = lax.rem(mine[k] + d, chip[k])
                first[k, d].wait_recv()
                q[k, at] = (pack_ref[k, c, at].astype(F32) + r0[k, at].astype(F32)).astype(BF16)
                if d:
                    second[k, d] = copy_to(
                        q.at[k, at], r1.at[k, mine[k]], (s1.at[k, d], v1.at[k, d]), peers[k](d)
                    )
                    copies.append(second[k, d])
    token_gradient(images, cot_ref, gain_ref, dtok_ref, nx_ref, inv_ref, alive_ref, dn_ref)
    for k in (0, 1):
        total = q[k, mine[k]].astype(F32)
        for d in ring_order(chip[k]):
            second[k, d].wait_recv()
            total = total + r1[k, lax.rem(mine[k] - d + chip[k], chip[k])].astype(F32)
        t_ref[:, k] = total.astype(BF16)
    third = {}
    for d in reversed(ring_order(nx)):
        third[d] = copy_to(t_ref.at[lax.rem(x + d, nx)], r2.at[x], (s2.at[d], v2.at[d]), x_peer(d))
        copies.append(third[d])
    total = t_ref[x].astype(F32)
    for d in ring_order(nx):
        third[d].wait_recv()
        total = total + r2[lax.rem(x - d + nx, nx)].astype(F32)
    u_ref[...] = total.astype(BF16)
    fourth = {}
    for k in (0, 1):
        n = chip[1 - k]
        for d in reversed(ring_order(n)):
            fourth[k, d] = copy_to(
                u_ref.at[k], r3.at[k, mine[1 - k]], (s3.at[k, d], v3.at[k, d]), peers[1 - k](d)
            )
            copies.append(fourth[k, d])
        r3[k, mine[1 - k]] = u_ref[k]
    fifth = {}
    for k in (0, 1):
        n = chip[1 - k]
        for d in ring_order(n):
            fourth[k, d].wait_recv()
        total = r3[k, 0].astype(F32)
        for i in range(1, n):
            total = total + r3[k, i].astype(F32)
        out_ref[k, c, mine[k], x] = total.astype(BF16)
        block = out_ref.at[k, c, mine[k], x]
        for d in reversed(ring_order(nx)):
            fifth[k, d] = copy_to(block, block, (s4.at[k, d], v4.at[k, d]), x_peer(d))
            copies.append(fifth[k, d])
    sixth = {}
    last = {}
    for k in (0, 1):
        for d in ring_order(nx):
            fifth[k, d].wait_recv()
        block = out_ref.at[k, c, mine[k]]
        for d in reversed(ring_order(chip[k])):
            sixth[k, d] = copy_to(block, block, (s5.at[k, d], v5.at[k, d]), peers[k](d))
            copies.append(sixth[k, d])
        last[k, 0] = copy_to(block, block, (s6.at[k, 0], v6.at[k, 0]), partner)
        copies.append(last[k, 0])
    orders = [ring_order(n) for n in chip]
    for step in range(max(chip) - 1):
        for k in (0, 1):
            if step < chip[k] - 1:
                d = orders[k][step]
                sixth[k, d].wait_recv()
                block = out_ref.at[k, c, lax.rem(mine[k] - d + chip[k], chip[k])]
                last[k, d] = copy_to(block, block, (s6.at[k, d], v6.at[k, d]), partner)
                copies.append(last[k, d])
    for copy in last.values():
        copy.wait_recv()
    for copy in copies:
        copy.wait_send()


def finish_kernel(dtok_ref, sum_ref, out_ref, wi_ref, bi_ref, wo_ref, bo_ref, gain_ref, shift_ref):
    out_ref[...] = dtok_ref[...]
    total = jnp.zeros((LINES, 128), F32)
    for k in (0, 1):
        for i in range(56 - 2 * k):
            piece = sum_ref[k, i].astype(F32)
            total = total + piece * piece
    total = jnp.sum(jnp.sum(total, axis=1, keepdims=True), axis=0, keepdims=True)
    factor = jnp.minimum(1.0, clip_share * math.sqrt(ENTRIES) / jnp.sqrt(total + 1e-06))
    for i in range(PMAX // LINES):
        for b in range(3):
            box = (slice(i * LINES, (i + 1) * LINES), slice(b * 128, (b + 1) * 128))
            wi_ref[box] = (sum_ref[0, i * 3 + b].astype(F32) * factor).astype(BF16)
            wo_ref[box] = (sum_ref[1, i * 3 + b].astype(F32) * factor).astype(BF16)
    one = sum_ref[0, 54].astype(F32) * factor
    two = sum_ref[0, 55].astype(F32) * factor
    for b in range(6):
        at = pl.ds(b * 128, 128)
        gain_ref[at] = one[b].astype(BF16)
        shift_ref[at] = one[6 + b].astype(BF16)
    for b in range(3):
        width = min(128, PMAX - b * 128)
        bi_ref[pl.ds(b * 128, 128)] = two[b].astype(BF16)
        bo_ref[pl.ds(b * 128, width)] = two[3 + b, :width].astype(BF16)


def main(nx, ny, nz, tokens, cotangent, patch_mask, image_tiles, patches, *weights):
    w_in, b_in, w_out, ln_gain, ln_shift = weights
    args = (image_tiles.T, patches.T, tokens, cotangent, patch_mask, w_in, b_in, w_out.T, ln_gain, ln_shift)
    n, places = max(ny, nz), image_tiles.shape[0]
    shape, dma = jax.ShapeDtypeStruct, pltpu.SemaphoreType.DMA
    block = (BLOCKS // (2 * n * nx) * LINES, 128)
    sems = [(2, n), (2, n), (nx,), (2, n), (2, nx), (2, n), (2, n)]
    return pl.pallas_call(
        lambda *refs: main_kernel(nx, ny, nz, *refs),
        name="main",
        out_shape=(shape((ROWS, C), BF16), shape((2, 2, n, nx, *block), BF16)),
        in_specs=[HBM] * 10,
        out_specs=(VMEM, VMEM),
        scratch_shapes=[
            pltpu.SMEM((3, places), jnp.int32),
            pltpu.SMEM((3, places), jnp.int32),
            pltpu.VMEM((ROWS, C), BF16),
            pltpu.VMEM((ROWS, C), BF16),
            pltpu.VMEM((ROWS,), jnp.int32),
            pltpu.VMEM((PMAX, H), BF16),
            pltpu.VMEM((H,), F32),
            pltpu.VMEM((PMAX, H), BF16),
            pltpu.VMEM((C,), F32),
            pltpu.VMEM((C,), F32),
            dma((10,)),
            pltpu.VMEM((ROWS, C), F32),
            pltpu.VMEM((ROWS, 128), F32),
            pltpu.VMEM((ROWS, 128), F32),
            pltpu.VMEM((PAD_TILES, TILE, C), BF16),
            pltpu.VMEM((PAD_TILES, TILE, C), BF16),
            pltpu.VMEM((sum(SPANS) // TILE, TILE, C), BF16),
            pltpu.VMEM((H, C), BF16),
            pltpu.VMEM((H, C), BF16),
            pltpu.VMEM((PMAX, H), F32),
            pltpu.VMEM((PMAX, H), F32),
            pltpu.VMEM((16, H), F32),
            pltpu.VMEM((2 * LINES, 128), F32),
            pltpu.VMEM((2, 2, n, nx, *block), BF16),
            pltpu.VMEM((2, n, nx, *block), BF16),
            pltpu.VMEM((2, n, nx, *block), BF16),
            pltpu.VMEM((2, n, nx, *block), BF16),
            pltpu.VMEM((nx, 2, *block), BF16),
            pltpu.VMEM((nx, 2, *block), BF16),
            pltpu.VMEM((2, *block), BF16),
            pltpu.VMEM((2, n, *block), BF16),
        ]
        + [dma(shape) for shape in sems for _ in range(2)],
        compiler_params=pltpu.CompilerParams(collective_id=0, has_side_effects=True, vmem_limit_bytes=20 << 20),
    )(*[pltpu.with_memory_space_constraint(v, pltpu.HBM) for v in args])


def finish(dtokens, sums):
    shape = jax.ShapeDtypeStruct
    shapes = ((ROWS, C), (PMAX, H), (H,), (PMAX, H), (PMAX,), (C,), (C,))
    return pl.pallas_call(
        finish_kernel,
        name="finish",
        out_shape=tuple(shape(s, BF16) for s in shapes),
        in_specs=[VMEM, VMEM],
        out_specs=(VMEM,) * 7,
        compiler_params=pltpu.CompilerParams(vmem_limit_bytes=10 << 20),
    )(dtokens, sums)


def solution(mesh):
    ny, nz = mesh.shape["dp"] // NX, mesh.shape["group"] // 2

    def local(*args):
        dtokens, sums = main(NX, ny, nz, *args)
        dtokens, w_in, b_in, w_out, b_out, gain, shift = finish(dtokens, sums.reshape(2, BLOCKS, LINES, 128))
        return (dtokens, w_in, b_in, w_out.T, b_out, gain, shift)

    rows = P(AXES, None)
    in_specs = (rows, rows, P(AXES)) + (P(),) * 7
    out_specs = (rows,) + (P(),) * 6
    return jax.shard_map(local, mesh=mesh, in_specs=in_specs, out_specs=out_specs, check_vma=False)
```

```python
import math

import jax
import jax.numpy as jnp
from jax import lax
from jax.experimental import pallas as pl
from jax.experimental.pallas import tpu as pltpu
from jax.sharding import PartitionSpec as P

PMAX = 288
TILE = 32
TILES = 10
ROWS = TILE * TILES
C = 768
H = 384
NX = 4
SPANS = (288, 160, 96)
BASES = (0, 9, 14)
PAD_TILES = TILES + PMAX // TILE
LINES = 16
BLOCKS = 64
ENTRIES = 2 * PMAX * H + H + PMAX + 2 * C

ln_epsilon = 1e-05
clip_share = 0.5
F32 = jnp.float32
BF16 = jnp.bfloat16
MESH = pl.DeviceIdType.MESH
AXES = ("dp", "group")
VMEM = pl.BlockSpec(memory_space=pltpu.VMEM)
HBM = pl.BlockSpec(memory_space=pltpu.HBM)


def dot(a, b, da, db):
    return lax.dot_general(a, b, (((da,), (db,)), ((), ())), preferred_element_type=F32)


def gelu_pair(preact):
    scaled = preact * 0.7071067811865476
    normal_cdf = 0.5 * lax.erf(scaled) + 0.5
    density = jnp.exp2(scaled * scaled * -1.4426950408889634)
    return (preact * normal_cdf, normal_cdf + preact * 0.3989422804014327 * density)


def wide(col):
    return jnp.concatenate([col] * (C // 128), axis=1)


def column(row):
    return jnp.transpose(jnp.broadcast_to(row, (128, row.shape[1])))


def image_table(tiles_ref, patches_ref, place):
    tiles = [tiles_ref[s, place] for s in range(3)]
    counts = [patches_ref[s, place] for s in range(3)]
    starts = [jnp.int32(0), tiles[0], tiles[0] + tiles[1]]
    images = list(zip(tiles, starts, counts))
    for i, j in ((0, 1), (0, 2), (1, 2)):
        a, b = images[i], images[j]
        swap = b[0] > a[0]
        images[i] = tuple(jnp.where(swap, q, p) for p, q in zip(a, b))
        images[j] = tuple(jnp.where(swap, p, q) for p, q in zip(a, b))
    return images


def rows_of(images, t, dn_ref, alive_ref):
    source = jnp.int32(0)
    for j, (tiles, start, _) in enumerate(images):
        held = (start <= t) & (t < start + tiles)
        source = jnp.where(held, BASES[j] + t - start, source)
    return dn_ref[source].astype(F32) * wide(alive_ref[t * TILE : (t + 1) * TILE, :])


def gradients(
    loads, tiles_ref, patches_ref, tok_ref, cot_ref, mask_ref, wi_ref, bi_ref, wo_ref, gain_ref, shift_ref, pack_ref,
    nx_ref, inv_ref, alive_ref, x_ref, d_ref, dn_ref, act_ref, dpre_ref, gi_ref, go_ref, bo_ref, small_ref,
    xs_ref, ds_ref, pre_ref, dz_ref, sum_ref, wt_ref, ro_ref, late_ref,
):
    place = lax.axis_index("dp") * lax.axis_size("group") + lax.axis_index("group")
    x_ref[TILES:] = jnp.zeros((PMAX // TILE, TILE, C), BF16)
    d_ref[TILES:] = jnp.zeros((PMAX // TILE, TILE, C), BF16)
    sum_ref[...] = jnp.zeros((H, 128), F32)
    ro_ref[TILES:] = jnp.zeros((PMAX // TILE, TILE, 128), F32)
    small_ref[...] = jnp.zeros((LINES, 128), F32)
    late_ref[...] = jnp.zeros((LINES, 128), F32)
    for load in loads[:6]:
        load.wait()
    images = image_table(tiles_ref, patches_ref, place)
    row = lax.broadcasted_iota(jnp.int32, (ROWS, 128), 0)
    alive = jnp.zeros((ROWS, 128), F32)
    for _, start, count in images:
        first = start * TILE
        alive = jnp.where((row >= first) & (row < first + count), 1.0, alive)
    alive_ref[...] = alive * column(mask_ref[...].astype(F32).reshape(1, ROWS))
    gain = gain_ref[...].reshape(1, C)
    shift = shift_ref[...].reshape(1, C)
    for t in range(TILES):
        rows = slice(t * TILE, (t + 1) * TILE)
        values = tok_ref[rows, :].astype(F32)
        center = values - jnp.mean(values, axis=1, keepdims=True)
        inv = lax.rsqrt(jnp.mean(center * center, axis=1, keepdims=True) + ln_epsilon)
        normal = center * inv
        nx_ref[rows, :] = normal
        inv_ref[rows, :] = jnp.broadcast_to(inv, (TILE, 128))
        x_ref[t] = ((normal * gain + shift) * wide(alive_ref[rows, :])).astype(BF16)
    for load in loads[6:]:
        load.wait()
    for t in range(TILES):
        rows = slice(t * TILE, (t + 1) * TILE)
        dout = (cot_ref[rows, :].astype(F32) * wide(alive_ref[rows, :])).astype(BF16)
        d_ref[t] = dout
        ro_ref[t] = jnp.broadcast_to(jnp.sum(dout.astype(F32), axis=1, keepdims=True), (TILE, 128))

    bias = column(bi_ref[...].reshape(1, H))
    bias = jnp.concatenate([bias, bias], axis=1)
    wt_ref[0] = jnp.transpose(wi_ref[...])
    wt_ref[1] = jnp.transpose(wo_ref[...])
    bo_ref[...] = jnp.zeros((H, 128), F32)

    def place_rows(j):
        tiles, start, _ = images[j]
        for u in range(SPANS[j] // TILE):
            held = jnp.where(u < tiles, 1.0, 0.0)
            keep = held.astype(BF16)
            bo_ref[u * TILE : (u + 1) * TILE, :] += ro_ref[start + u] * held
            at = slice((BASES[j] + u) * TILE, (BASES[j] + u + 1) * TILE)
            xs_ref[at, :] = x_ref[start + u] * keep
            ds_ref[at, :] = d_ref[start + u] * keep

    def own(j):
        return slice(BASES[j] * TILE, BASES[j] * TILE + SPANS[j])

    def project(j, part):
        cols = slice(part * 256, (part + 1) * 256)
        pre_ref[j % 2, :, cols] = dot(wt_ref[0, :, : SPANS[j]], xs_ref[own(j), cols], 1, 0)
        dz_ref[j % 2, :, cols] = dot(wt_ref[1, :, : SPANS[j]], ds_ref[own(j), cols], 1, 0)

    def activate(j, part):
        cols = slice(part * 256, (part + 1) * 256)
        act, slope = gelu_pair(pre_ref[j % 2, :, cols] + bias)
        act_ref[j, :, cols] = act.astype(BF16)
        dpre = dz_ref[j % 2, :, cols] * slope
        dpre_ref[j, :, cols] = dpre.astype(BF16)
        sum_ref[...] += dpre[:, :128] + dpre[:, 128:]

    def reduce(j, part):
        span = SPANS[j]
        if part == 0:
            gi = dot(xs_ref[own(j), :], dpre_ref[j], 1, 1)
            gi_ref[:span, :] = gi if j == 0 else gi_ref[:span, :] + gi
        elif part == 1:
            go = dot(ds_ref[own(j), :], act_ref[j], 1, 1)
            go_ref[:span, :] = go if j == 0 else go_ref[:span, :] + go

    for j in range(3):
        place_rows(j)
    for step in range(5):
        for part in range(3):
            if step < 3:
                project(step, part)
            if 1 <= step < 4:
                activate(step - 1, part)
            if step >= 2:
                reduce(step - 2, part)

    for b in range(3):
        small_ref[b : b + 1, :] = jnp.sum(jnp.transpose(sum_ref[b * 128 : (b + 1) * 128, :]), axis=0, keepdims=True)
        small_ref[3 + b : 4 + b, :] = jnp.transpose(bo_ref[b * 128 : (b + 1) * 128, :])[0:1]
    n, nx, lines = pack_ref.shape[2:5]
    each = lines // LINES

    def put(k, i, value):
        shard, at = i // each, i % each * LINES
        pack_ref[k, shard // (n * nx), shard // nx % n, shard % nx, at : at + LINES] = value

    for i in range(PMAX // LINES):
        for b in range(3):
            box = (slice(i * LINES, (i + 1) * LINES), slice(b * 128, (b + 1) * 128))
            put(0, i * 3 + b, gi_ref[box].astype(BF16))
            put(1, i * 3 + b, go_ref[box].astype(BF16))
    put(0, 54, small_ref[...].astype(BF16))
    for k, used in ((0, 55), (1, 54)):
        for i in range(used, BLOCKS):
            put(k, i, jnp.zeros((LINES, 128), BF16))
    return images


def late_sums(images, wi_ref, dpre_ref, dn_ref, nx_ref, alive_ref, late_ref, bl_ref):
    for j in range(3):
        back_rows = dot(wi_ref[: SPANS[j], :], dpre_ref[j], 1, 0).astype(BF16)
        for u in range(SPANS[j] // TILE):
            dn_ref[BASES[j] + u] = back_rows[u * TILE : (u + 1) * TILE]
    gain_sum = jnp.zeros((8, C), F32)
    shift_sum = jnp.zeros((8, C), F32)
    for t in range(TILES):
        d_rows = rows_of(images, t, dn_ref, alive_ref)
        weighted = d_rows * nx_ref[t * TILE : (t + 1) * TILE, :]
        for i in range(0, TILE, 8):
            gain_sum = gain_sum + weighted[i : i + 8]
            shift_sum = shift_sum + d_rows[i : i + 8]

    gain_row = jnp.sum(gain_sum, axis=0, keepdims=True)
    shift_row = jnp.sum(shift_sum, axis=0, keepdims=True)
    for b in range(6):
        late_ref[b : b + 1, :] = gain_row[:, b * 128 : (b + 1) * 128]
        late_ref[6 + b : 7 + b, :] = shift_row[:, b * 128 : (b + 1) * 128]
    bl_ref[...] = late_ref[...].astype(BF16)


def token_gradient(images, cot_ref, gain_ref, dtok_ref, nx_ref, inv_ref, alive_ref, dn_ref):
    gain = gain_ref[...].reshape(1, C)
    for t in range(TILES):
        rows = slice(t * TILE, (t + 1) * TILE)
        normal = nx_ref[rows, :]
        scaled = rows_of(images, t, dn_ref, alive_ref) * gain
        inner = jnp.mean(scaled * normal, axis=1, keepdims=True)
        d_norm = (scaled - jnp.mean(scaled, axis=1, keepdims=True) - normal * inner) * wide(inv_ref[rows, :])
        dtok_ref[rows, :] = (cot_ref[rows, :].astype(F32) + d_norm).astype(BF16)


def ring_order(n):
    order = []
    for d in range(1, n // 2 + 1):
        order.append(d)
        if n - d != d:
            order.append(n - d)
    return order


def main_kernel(
    nx, ny, nz,
    tiles_in, patches_in, tok_in, cot_in, mask_in, wi_in, bi_in, wo_in, gain_in, shift_in,
    dtok_ref, out_ref, late_out,
    tiles_ref, patches_ref, tok_ref, cot_ref, mask_ref, wi_ref, bi_ref, wo_ref, gain_ref, shift_ref, in_sem,
    nx_ref, inv_ref, alive_ref, x_ref, d_ref, dn_ref, act_ref, dpre_ref, gi_ref, go_ref, bo_ref, small_ref,
    xs_ref, ds_ref, pre_ref, dz_ref, sum_ref, wt_ref, ro_ref, late_ref,
    bl_ref, lc, lz, lx, ly, sl, vl,
    pack_ref, r0, q, r1, t_ref, r2, u_ref, r3,
    s0, v0, s1, v1, s2, v2, s3, v3, s4, v4, s5, v5, s6, v6,
):
    pairs = (
        (tok_in, tok_ref), (mask_in, mask_ref), (gain_in, gain_ref), (shift_in, shift_ref), (tiles_in, tiles_ref),
        (patches_in, patches_ref), (cot_in, cot_ref), (wi_in, wi_ref), (wo_in, wo_ref), (bi_in, bi_ref),
    )
    loads = [pltpu.make_async_copy(a, b, in_sem.at[i]) for i, (a, b) in enumerate(pairs)]
    for load in loads:
        load.start()
    dp = lax.axis_index("dp")
    group = lax.axis_index("group")
    y, x = dp // nx, lax.rem(dp, nx)
    z, c = group // 2, lax.rem(group, 2)
    mate = 1 - c
    chip = (nz, ny)
    mine = (z, y)
    partner = (dp, z * 2 + mate)

    def z_peer(d):
        return (dp, lax.rem(z + d, nz) * 2 + c)

    def y_peer(d):
        return (lax.rem(y + d, ny) * nx + x, group)

    def x_peer(d):
        return (y * nx + lax.rem(x + d, nx), group)

    peers = (z_peer, y_peer)
    barrier = pltpu.get_barrier_semaphore()
    everyone = [partner]
    everyone += [z_peer(d) for d in range(1, nz)]
    everyone += [y_peer(d) for d in range(1, ny)]
    everyone += [x_peer(d) for d in range(1, nx)]
    for device in everyone:
        pl.semaphore_signal(barrier, inc=1, device_id=device, device_id_type=MESH)
    images = gradients(
        loads, tiles_ref, patches_ref, tok_ref, cot_ref, mask_ref, wi_ref, bi_ref, wo_ref, gain_ref, shift_ref, pack_ref,
        nx_ref, inv_ref, alive_ref, x_ref, d_ref, dn_ref, act_ref, dpre_ref, gi_ref, go_ref, bo_ref, small_ref,
        xs_ref, ds_ref, pre_ref, dz_ref, sum_ref, wt_ref, ro_ref, late_ref,
    )
    pl.semaphore_wait(barrier, len(everyone))
    def send(source, target, send_sem, recv_sem, device):
        copy = pltpu.make_async_remote_copy(
            src_ref=source, dst_ref=target, send_sem=send_sem, recv_sem=recv_sem, device_id=device, device_id_type=MESH
        )
        copy.start()
        return copy

    def drain(ref, sem):
        pltpu.make_async_copy(ref, ref, sem).wait()

    def back(at, d, n):
        return lax.rem(at - d + n, n)

    places = ((lc, 2, c, lambda d: partner), (lz, nz, z, z_peer), (lx, nx, x, x_peer), (ly, ny, y, y_peer))

    def late_send(stage):
        slots, n, at, peer = places[stage]
        for d in reversed(ring_order(n)):
            send(bl_ref.at[stage], slots.at[at], sl.at[stage], vl.at[stage], peer(d))
        slots[at] = bl_ref[stage]

    def late_wait(stage):
        slots, n, _, _ = places[stage]
        drain(slots.at[pl.ds(0, n - 1)], vl.at[stage])
        total = slots[0].astype(F32)
        for i in range(1, n):
            total = total + slots[i].astype(F32)
        return total.astype(BF16)

    near = ring_order(nx)
    rings = [ring_order(m) for m in chip]
    rest = [pl.ds(0, m - 1) for m in chip]
    orders = [ring[::-1] + [0] for ring in rings]
    steps = [(k, orders[k][i]) for i in range(max(chip)) for k in (0, 1) if i < chip[k]]
    first = {}
    for k, d in steps:
        at = lax.rem(mine[k] + d, chip[k])
        first[k, d] = send(pack_ref.at[k, mate, at], r0.at[k, at], s0.at[k], v0.at[k, d], partner)
    for k, d in steps:
        at = lax.rem(mine[k] + d, chip[k])
        first[k, d].wait_recv()
        q[k, at] = (pack_ref[k, c, at].astype(F32) + r0[k, at].astype(F32)).astype(BF16)
        if d:
            send(q.at[k, at], r1.at[k, mine[k]], s1.at[k], v1.at[k], peers[k](d))
    late_sums(images, wi_ref, dpre_ref, dn_ref, nx_ref, alive_ref, late_ref, bl_ref.at[0])
    late_send(0)
    token_gradient(images, cot_ref, gain_ref, dtok_ref, nx_ref, inv_ref, alive_ref, dn_ref)
    for k in (0, 1):
        drain(r1.at[k, rest[k]], v1.at[k])
        total = q[k, mine[k]].astype(F32)
        for d in rings[k]:
            total = total + r1[k, back(mine[k], d, chip[k])].astype(F32)
        t_ref[:, k] = total.astype(BF16)
    for d in near[::-1]:
        send(t_ref.at[lax.rem(x + d, nx)], r2.at[x], s2.at[0], v2.at[0], x_peer(d))
    bl_ref[1] = late_wait(0)
    late_send(1)
    drain(r2.at[pl.ds(0, nx - 1)], v2.at[0])
    total = t_ref[x].astype(F32)
    for d in near:
        total = total + r2[back(x, d, nx)].astype(F32)
    u_ref[...] = total.astype(BF16)
    for k in (0, 1):
        for d in rings[1 - k][::-1]:
            send(u_ref.at[k], r3.at[k, mine[1 - k]], s3.at[k], v3.at[k], peers[1 - k](d))
        r3[k, mine[1 - k]] = u_ref[k]
    bl_ref[2] = late_wait(1)
    late_send(2)
    for k in (0, 1):
        drain(r3.at[k, rest[1 - k]], v3.at[k])
        total = r3[k, 0].astype(F32)
        for i in range(1, chip[1 - k]):
            total = total + r3[k, i].astype(F32)
        out_ref[k, c, mine[k], x] = total.astype(BF16)
        block = out_ref.at[k, c, mine[k], x]
        for d in near[::-1]:
            send(block, block, s4.at[k], v4.at[k], x_peer(d))
    bl_ref[3] = late_wait(2)
    late_send(3)
    sixth = {}
    for k in (0, 1):
        drain(out_ref.at[k, c, mine[k], pl.ds(0, nx - 1)], v4.at[k])
        block = out_ref.at[k, c, mine[k]]
        for d in rings[k]:
            sixth[k, d] = send(block, block, s5.at[k], v5.at[k, d], peers[k](d))
        send(block, block, s6.at[k], v6.at[k], partner)
    for i in range(max(chip) - 1):
        for k in (0, 1):
            if i < chip[k] - 1:
                d = rings[k][i]
                sixth[k, d].wait_recv()
                block = out_ref.at[k, c, back(mine[k], d, chip[k])]
                send(block, block, s6.at[k], v6.at[k], partner)
    late_out[...] = late_wait(3)
    for k in (0, 1):
        drain(out_ref.at[k, mate], v6.at[k])
        drain(pack_ref.at[k, mate], s0.at[k])
        drain(q.at[k, rest[k]], s1.at[k])
        drain(r3.at[k, rest[1 - k]], s3.at[k])
        drain(out_ref.at[k, c, mine[k], pl.ds(0, nx - 1)], s4.at[k])
        drain(q.at[k, rest[k]], s5.at[k])
        drain(out_ref.at[k, c], s6.at[k])
    drain(r2.at[pl.ds(0, nx - 1)], s2.at[0])
    for stage, (slots, n, _, _) in enumerate(places):
        drain(slots.at[pl.ds(0, n - 1)], sl.at[stage])


def finish_kernel(dtok_ref, sum_ref, late_ref, out_ref, wi_ref, bi_ref, wo_ref, bo_ref, gain_ref, shift_ref, sem):
    move = pltpu.make_async_copy(dtok_ref, out_ref, sem)
    move.start()
    one = late_ref[...].astype(F32)
    total = one * one
    for k in (0, 1):
        for i in range(55 - k):
            piece = sum_ref[k, i].astype(F32)
            total = total + piece * piece
    total = jnp.sum(jnp.sum(total, axis=1, keepdims=True), axis=0, keepdims=True)
    factor = jnp.minimum(1.0, clip_share * math.sqrt(ENTRIES) / jnp.sqrt(total + 1e-06))
    for i in range(PMAX // LINES):
        for b in range(3):
            box = (slice(i * LINES, (i + 1) * LINES), slice(b * 128, (b + 1) * 128))
            wi_ref[box] = (sum_ref[0, i * 3 + b].astype(F32) * factor).astype(BF16)
            wo_ref[box] = (sum_ref[1, i * 3 + b].astype(F32) * factor).astype(BF16)
    one = one * factor
    two = sum_ref[0, 54].astype(F32) * factor
    for b in range(6):
        at = pl.ds(b * 128, 128)
        gain_ref[at] = one[b].astype(BF16)
        shift_ref[at] = one[6 + b].astype(BF16)
    for b in range(3):
        width = min(128, PMAX - b * 128)
        bi_ref[pl.ds(b * 128, 128)] = two[b].astype(BF16)
        bo_ref[pl.ds(b * 128, width)] = two[3 + b, :width].astype(BF16)
    move.wait()


def main(nx, ny, nz, tokens, cotangent, patch_mask, image_tiles, patches, *weights):
    w_in, b_in, w_out, ln_gain, ln_shift = weights
    args = (image_tiles.T, patches.T, tokens, cotangent, patch_mask, w_in, b_in, w_out.T, ln_gain, ln_shift)
    n, places = max(ny, nz), image_tiles.shape[0]
    shape, dma = jax.ShapeDtypeStruct, pltpu.SemaphoreType.DMA
    block = (BLOCKS // (2 * n * nx) * LINES, 128)
    sems = [(2,), (2, n), (2,), (2,), (1,), (1,), (2,), (2,), (2,), (2,), (2,), (2, n), (2,), (2,)]
    return pl.pallas_call(
        lambda *refs: main_kernel(nx, ny, nz, *refs),
        name="main",
        out_shape=(shape((ROWS, C), BF16), shape((2, 2, n, nx, *block), BF16), shape((LINES, 128), BF16)),
        in_specs=[HBM] * 10,
        out_specs=(VMEM, VMEM, VMEM),
        scratch_shapes=[
            pltpu.SMEM((3, places), jnp.int32),
            pltpu.SMEM((3, places), jnp.int32),
            pltpu.VMEM((ROWS, C), BF16),
            pltpu.VMEM((ROWS, C), BF16),
            pltpu.VMEM((ROWS,), jnp.int32),
            pltpu.VMEM((PMAX, H), BF16),
            pltpu.VMEM((H,), F32),
            pltpu.VMEM((PMAX, H), BF16),
            pltpu.VMEM((C,), F32),
            pltpu.VMEM((C,), F32),
            dma((10,)),
            pltpu.VMEM((ROWS, C), F32),
            pltpu.VMEM((ROWS, 128), F32),
            pltpu.VMEM((ROWS, 128), F32),
            pltpu.VMEM((PAD_TILES, TILE, C), BF16),
            pltpu.VMEM((PAD_TILES, TILE, C), BF16),
            pltpu.VMEM((sum(SPANS) // TILE, TILE, C), BF16),
            pltpu.VMEM((3, H, C), BF16),
            pltpu.VMEM((3, H, C), BF16),
            pltpu.VMEM((PMAX, H), F32),
            pltpu.VMEM((PMAX, H), F32),
            pltpu.VMEM((H, 128), F32),
            pltpu.VMEM((LINES, 128), F32),
            pltpu.VMEM((sum(SPANS), C), BF16),
            pltpu.VMEM((sum(SPANS), C), BF16),
            pltpu.VMEM((2, H, C), F32),
            pltpu.VMEM((2, H, C), F32),
            pltpu.VMEM((H, 128), F32),
            pltpu.VMEM((2, H, PMAX), BF16),
            pltpu.VMEM((PAD_TILES, TILE, 128), F32),
            pltpu.VMEM((LINES, 128), F32),
            pltpu.VMEM((4, LINES, 128), BF16),
            pltpu.VMEM((2, LINES, 128), BF16),
            pltpu.VMEM((nz, LINES, 128), BF16),
            pltpu.VMEM((nx, LINES, 128), BF16),
            pltpu.VMEM((ny, LINES, 128), BF16),
            dma((4,)),
            dma((4,)),
            pltpu.VMEM((2, 2, n, nx, *block), BF16),
            pltpu.VMEM((2, n, nx, *block), BF16),
            pltpu.VMEM((2, n, nx, *block), BF16),
            pltpu.VMEM((2, n, nx, *block), BF16),
            pltpu.VMEM((nx, 2, *block), BF16),
            pltpu.VMEM((nx, 2, *block), BF16),
            pltpu.VMEM((2, *block), BF16),
            pltpu.VMEM((2, n, *block), BF16),
        ]
        + [dma(shape) for shape in sems],
        compiler_params=pltpu.CompilerParams(collective_id=0, has_side_effects=True, vmem_limit_bytes=24 << 20),
    )(*[pltpu.with_memory_space_constraint(v, pltpu.HBM) for v in args])


def finish(dtokens, sums, late):
    shape = jax.ShapeDtypeStruct
    shapes = ((ROWS, C), (PMAX, H), (H,), (PMAX, H), (PMAX,), (C,), (C,))
    return pl.pallas_call(
        finish_kernel,
        name="finish",
        out_shape=tuple(shape(s, BF16) for s in shapes),
        in_specs=[VMEM] * 3,
        out_specs=(HBM,) + (VMEM,) * 6,
        scratch_shapes=[pltpu.SemaphoreType.DMA],
        compiler_params=pltpu.CompilerParams(vmem_limit_bytes=10 << 20),
    )(dtokens, sums, late)


def solution(mesh):
    ny, nz = mesh.shape["dp"] // NX, mesh.shape["group"] // 2

    def local(*args):
        dtokens, sums, late = main(NX, ny, nz, *args)
        dtokens, w_in, b_in, w_out, b_out, gain, shift = finish(
            dtokens, sums.reshape(2, BLOCKS, LINES, 128), late
        )
        return (dtokens, w_in, b_in, w_out.T, b_out, gain, shift)

    rows = P(AXES, None)
    in_specs = (rows, rows, P(AXES)) + (P(),) * 7
    out_specs = (rows,) + (P(),) * 6
    return jax.shard_map(local, mesh=mesh, in_specs=in_specs, out_specs=out_specs, check_vma=False)
```

```python
import math

import jax
import jax.numpy as jnp
from jax import lax
from jax.experimental import pallas as pl
from jax.experimental.pallas import tpu as pltpu
from jax.sharding import PartitionSpec as P

PMAX = 288
TILE = 32
TILES = 10
ROWS = TILE * TILES
C = 768
H = 384
NX = 4
SPANS = (288, 160, 96)
BASES = (0, 9, 14)
PAD_TILES = TILES + PMAX // TILE
LINES = 16
BLOCKS = 64
ENTRIES = 2 * PMAX * H + H + PMAX + 2 * C

ln_epsilon = 1e-05
clip_share = 0.5
F32 = jnp.float32
BF16 = jnp.bfloat16
MESH = pl.DeviceIdType.MESH
AXES = ("dp", "group")
VMEM = pl.BlockSpec(memory_space=pltpu.VMEM)
HBM = pl.BlockSpec(memory_space=pltpu.HBM)


def dot(a, b, da, db):
    return lax.dot_general(a, b, (((da,), (db,)), ((), ())), preferred_element_type=F32)


def gelu_pair(preact):
    scaled = preact * 0.7071067811865476
    normal_cdf = 0.5 * lax.erf(scaled) + 0.5
    density = jnp.exp2(scaled * scaled * -1.4426950408889634)
    return (preact * normal_cdf, normal_cdf + preact * 0.3989422804014327 * density)


def wide(col):
    return jnp.concatenate([col] * (C // 128), axis=1)


def column(row):
    return jnp.transpose(jnp.broadcast_to(row, (128, row.shape[1])))


def image_table(tiles_ref, patches_ref, place):
    tiles = [tiles_ref[s, place] for s in range(3)]
    counts = [patches_ref[s, place] for s in range(3)]
    starts = [jnp.int32(0), tiles[0], tiles[0] + tiles[1]]
    images = list(zip(tiles, starts, counts))
    for i, j in ((0, 1), (0, 2), (1, 2)):
        a, b = images[i], images[j]
        swap = b[0] > a[0]
        images[i] = tuple(jnp.where(swap, q, p) for p, q in zip(a, b))
        images[j] = tuple(jnp.where(swap, p, q) for p, q in zip(a, b))
    return images


def rows_of(images, t, dn_ref, alive_ref):
    source = jnp.int32(0)
    for j, (tiles, start, _) in enumerate(images):
        held = (start <= t) & (t < start + tiles)
        source = jnp.where(held, BASES[j] + t - start, source)
    return dn_ref[source].astype(F32) * wide(alive_ref[t * TILE : (t + 1) * TILE, :])


def gradients(
    loads, tiles_ref, patches_ref, tok_ref, cot_ref, mask_ref, wi_ref, bi_ref, wo_ref, gain_ref, shift_ref, pack_ref,
    nx_ref, inv_ref, alive_ref, x_ref, d_ref, dn_ref, act_ref, dpre_ref, gi_ref, go_ref, bo_ref, small_ref,
    xs_ref, ds_ref, pre_ref, dz_ref, sum_ref, wt_ref, ro_ref, late_ref,
):
    place = lax.axis_index("dp") * lax.axis_size("group") + lax.axis_index("group")
    x_ref[TILES:] = jnp.zeros((PMAX // TILE, TILE, C), BF16)
    d_ref[TILES:] = jnp.zeros((PMAX // TILE, TILE, C), BF16)
    sum_ref[...] = jnp.zeros((H, 128), F32)
    ro_ref[TILES:] = jnp.zeros((PMAX // TILE, TILE, 128), F32)
    small_ref[...] = jnp.zeros((LINES, 128), F32)
    late_ref[...] = jnp.zeros((LINES, 128), F32)
    for load in loads[:6]:
        load.wait()
    images = image_table(tiles_ref, patches_ref, place)
    row = lax.broadcasted_iota(jnp.int32, (ROWS, 128), 0)
    alive = jnp.zeros((ROWS, 128), F32)
    for _, start, count in images:
        first = start * TILE
        alive = jnp.where((row >= first) & (row < first + count), 1.0, alive)
    alive_ref[...] = alive * column(mask_ref[...].astype(F32).reshape(1, ROWS))
    gain = gain_ref[...].reshape(1, C)
    shift = shift_ref[...].reshape(1, C)
    for t in range(TILES):
        rows = slice(t * TILE, (t + 1) * TILE)
        values = tok_ref[rows, :].astype(F32)
        center = values - jnp.mean(values, axis=1, keepdims=True)
        inv = lax.rsqrt(jnp.mean(center * center, axis=1, keepdims=True) + ln_epsilon)
        normal = center * inv
        nx_ref[rows, :] = normal
        inv_ref[rows, :] = jnp.broadcast_to(inv, (TILE, 128))
        x_ref[t] = ((normal * gain + shift) * wide(alive_ref[rows, :])).astype(BF16)
    for load in loads[6:]:
        load.wait()
    for t in range(TILES):
        rows = slice(t * TILE, (t + 1) * TILE)
        dout = (cot_ref[rows, :].astype(F32) * wide(alive_ref[rows, :])).astype(BF16)
        d_ref[t] = dout
        ro_ref[t] = jnp.broadcast_to(jnp.sum(dout.astype(F32), axis=1, keepdims=True), (TILE, 128))

    bias = column(bi_ref[...].reshape(1, H))
    bias = jnp.concatenate([bias, bias], axis=1)
    wt_ref[0] = jnp.transpose(wi_ref[...])
    wt_ref[1] = jnp.transpose(wo_ref[...])
    bo_ref[...] = jnp.zeros((H, 128), F32)

    def place_rows(j):
        tiles, start, _ = images[j]
        for u in range(SPANS[j] // TILE):
            held = jnp.where(u < tiles, 1.0, 0.0)
            keep = held.astype(BF16)
            bo_ref[u * TILE : (u + 1) * TILE, :] += ro_ref[start + u] * held
            at = slice((BASES[j] + u) * TILE, (BASES[j] + u + 1) * TILE)
            xs_ref[at, :] = x_ref[start + u] * keep
            ds_ref[at, :] = d_ref[start + u] * keep

    def own(j):
        return slice(BASES[j] * TILE, BASES[j] * TILE + SPANS[j])

    def project(j, part):
        cols = slice(part * 256, (part + 1) * 256)
        pre_ref[j % 2, :, cols] = dot(wt_ref[0, :, : SPANS[j]], xs_ref[own(j), cols], 1, 0)
        dz_ref[j % 2, :, cols] = dot(wt_ref[1, :, : SPANS[j]], ds_ref[own(j), cols], 1, 0)

    def activate(j, part):
        cols = slice(part * 256, (part + 1) * 256)
        act, slope = gelu_pair(pre_ref[j % 2, :, cols] + bias)
        act_ref[j, :, cols] = act.astype(BF16)
        dpre = dz_ref[j % 2, :, cols] * slope
        dpre_ref[j, :, cols] = dpre.astype(BF16)
        sum_ref[...] += dpre[:, :128] + dpre[:, 128:]

    def reduce(j, part):
        span = SPANS[j]
        if part == 0:
            gi = dot(xs_ref[own(j), :], dpre_ref[j], 1, 1)
            gi_ref[:span, :] = gi if j == 0 else gi_ref[:span, :] + gi
        elif part == 1:
            go = dot(ds_ref[own(j), :], act_ref[j], 1, 1)
            go_ref[:span, :] = go if j == 0 else go_ref[:span, :] + go

    for j in range(3):
        place_rows(j)
    for step in range(5):
        for part in range(3):
            if step < 3:
                project(step, part)
            if 1 <= step < 4:
                activate(step - 1, part)
            if step >= 2:
                reduce(step - 2, part)

    for b in range(3):
        small_ref[b : b + 1, :] = jnp.sum(jnp.transpose(sum_ref[b * 128 : (b + 1) * 128, :]), axis=0, keepdims=True)
        small_ref[3 + b : 4 + b, :] = jnp.transpose(bo_ref[b * 128 : (b + 1) * 128, :])[0:1]
    n, nx, lines = pack_ref.shape[2:5]
    each = lines // LINES

    def put(k, i, value):
        shard, at = i // each, i % each * LINES
        pack_ref[k, shard // (n * nx), shard // nx % n, shard % nx, at : at + LINES] = value

    for i in range(PMAX // LINES):
        for b in range(3):
            box = (slice(i * LINES, (i + 1) * LINES), slice(b * 128, (b + 1) * 128))
            put(0, i * 3 + b, gi_ref[box].astype(BF16))
            put(1, i * 3 + b, go_ref[box].astype(BF16))
    put(0, 54, small_ref[...].astype(BF16))
    for k, used in ((0, 55), (1, 54)):
        for i in range(used, BLOCKS):
            put(k, i, jnp.zeros((LINES, 128), BF16))
    return images


def late_sums(images, wi_ref, dpre_ref, dn_ref, nx_ref, alive_ref, late_ref, bl_ref):
    for j in range(3):
        back_rows = dot(wi_ref[: SPANS[j], :], dpre_ref[j], 1, 0).astype(BF16)
        for u in range(SPANS[j] // TILE):
            dn_ref[BASES[j] + u] = back_rows[u * TILE : (u + 1) * TILE]
    gain_sum = jnp.zeros((8, C), F32)
    shift_sum = jnp.zeros((8, C), F32)
    for t in range(TILES):
        d_rows = rows_of(images, t, dn_ref, alive_ref)
        weighted = d_rows * nx_ref[t * TILE : (t + 1) * TILE, :]
        for i in range(0, TILE, 8):
            gain_sum = gain_sum + weighted[i : i + 8]
            shift_sum = shift_sum + d_rows[i : i + 8]

    gain_row = jnp.sum(gain_sum, axis=0, keepdims=True)
    shift_row = jnp.sum(shift_sum, axis=0, keepdims=True)
    for b in range(6):
        late_ref[b : b + 1, :] = gain_row[:, b * 128 : (b + 1) * 128]
        late_ref[6 + b : 7 + b, :] = shift_row[:, b * 128 : (b + 1) * 128]
    bl_ref[...] = late_ref[...].astype(BF16)


def token_gradient(images, cot_ref, gain_ref, dtok_ref, nx_ref, inv_ref, alive_ref, dn_ref):
    gain = gain_ref[...].reshape(1, C)
    for t in range(TILES):
        rows = slice(t * TILE, (t + 1) * TILE)
        normal = nx_ref[rows, :]
        scaled = rows_of(images, t, dn_ref, alive_ref) * gain
        inner = jnp.mean(scaled * normal, axis=1, keepdims=True)
        d_norm = (scaled - jnp.mean(scaled, axis=1, keepdims=True) - normal * inner) * wide(inv_ref[rows, :])
        dtok_ref[rows, :] = (cot_ref[rows, :].astype(F32) + d_norm).astype(BF16)


def ring_order(n):
    order = []
    for d in range(1, n // 2 + 1):
        order.append(d)
        if n - d != d:
            order.append(n - d)
    return order


def main_kernel(
    nx, ny, nz,
    tiles_in, patches_in, tok_in, cot_in, mask_in, wi_in, bi_in, wo_in, gain_in, shift_in,
    dtok_ref, out_ref, late_out,
    tiles_ref, patches_ref, tok_ref, cot_ref, mask_ref, wi_ref, bi_ref, wo_ref, gain_ref, shift_ref, in_sem,
    nx_ref, inv_ref, alive_ref, x_ref, d_ref, dn_ref, act_ref, dpre_ref, gi_ref, go_ref, bo_ref, small_ref,
    xs_ref, ds_ref, pre_ref, dz_ref, sum_ref, wt_ref, ro_ref, late_ref,
    bl_ref, lc, lz, lx, ly, sl, vl,
    pack_ref, r0, q, r1, t_ref, r2, u_ref, r3,
    s0, v0, s1, v1, s2, v2, s3, v3, s4, v4, s5, v5, s6, v6,
):
    pairs = (
        (tok_in, tok_ref), (mask_in, mask_ref), (gain_in, gain_ref), (shift_in, shift_ref), (tiles_in, tiles_ref),
        (patches_in, patches_ref), (cot_in, cot_ref), (wi_in, wi_ref), (wo_in, wo_ref), (bi_in, bi_ref),
    )
    loads = [pltpu.make_async_copy(a, b, in_sem.at[i]) for i, (a, b) in enumerate(pairs)]
    for load in loads:
        load.start()
    dp = lax.axis_index("dp")
    group = lax.axis_index("group")
    y, x = dp // nx, lax.rem(dp, nx)
    z, c = group // 2, lax.rem(group, 2)
    mate = 1 - c
    chip = (nz, ny)
    mine = (z, y)
    partner = (dp, z * 2 + mate)

    def z_peer(d):
        return (dp, lax.rem(z + d, nz) * 2 + c)

    def y_peer(d):
        return (lax.rem(y + d, ny) * nx + x, group)

    def x_peer(d):
        return (y * nx + lax.rem(x + d, nx), group)

    peers = (z_peer, y_peer)
    barrier = pltpu.get_barrier_semaphore()
    everyone = [partner]
    everyone += [z_peer(d) for d in range(1, nz)]
    everyone += [y_peer(d) for d in range(1, ny)]
    everyone += [x_peer(d) for d in range(1, nx)]
    for device in everyone:
        pl.semaphore_signal(barrier, inc=1, device_id=device, device_id_type=MESH)
    images = gradients(
        loads, tiles_ref, patches_ref, tok_ref, cot_ref, mask_ref, wi_ref, bi_ref, wo_ref, gain_ref, shift_ref, pack_ref,
        nx_ref, inv_ref, alive_ref, x_ref, d_ref, dn_ref, act_ref, dpre_ref, gi_ref, go_ref, bo_ref, small_ref,
        xs_ref, ds_ref, pre_ref, dz_ref, sum_ref, wt_ref, ro_ref, late_ref,
    )
    pl.semaphore_wait(barrier, len(everyone))
    def send(source, target, send_sem, recv_sem, device):
        copy = pltpu.make_async_remote_copy(
            src_ref=source, dst_ref=target, send_sem=send_sem, recv_sem=recv_sem, device_id=device, device_id_type=MESH
        )
        copy.start()
        return copy

    def drain(ref, sem):
        pltpu.make_async_copy(ref, ref, sem).wait()

    def back(at, d, n):
        return lax.rem(at - d + n, n)

    places = ((lc, 2, c, lambda d: partner), (lz, nz, z, z_peer), (lx, nx, x, x_peer), (ly, ny, y, y_peer))

    def late_send(stage):
        slots, n, at, peer = places[stage]
        for d in reversed(ring_order(n)):
            send(bl_ref.at[stage], slots.at[at], sl.at[stage], vl.at[stage], peer(d))
        slots[at] = bl_ref[stage]

    def late_wait(stage):
        slots, n, _, _ = places[stage]
        drain(slots.at[pl.ds(0, n - 1)], vl.at[stage])
        total = slots[0].astype(F32)
        for i in range(1, n):
            total = total + slots[i].astype(F32)
        return total.astype(BF16)

    near = ring_order(nx)
    rings = [ring_order(m) for m in chip]
    rest = [pl.ds(0, m - 1) for m in chip]
    orders = [ring[::-1] + [0] for ring in rings]
    steps = [(k, orders[k][i]) for i in range(max(chip)) for k in (0, 1) if i < chip[k]]
    first = {}
    for k, d in steps:
        at = lax.rem(mine[k] + d, chip[k])
        first[k, d] = send(pack_ref.at[k, mate, at], r0.at[k, at], s0.at[k], v0.at[k, d], partner)
    for k, d in steps:
        at = lax.rem(mine[k] + d, chip[k])
        first[k, d].wait_recv()
        q[k, at] = (pack_ref[k, c, at].astype(F32) + r0[k, at].astype(F32)).astype(BF16)
        if d:
            send(q.at[k, at], r1.at[k, mine[k]], s1.at[k], v1.at[k], peers[k](d))
    late_sums(images, wi_ref, dpre_ref, dn_ref, nx_ref, alive_ref, late_ref, bl_ref.at[0])
    late_send(0)
    token_gradient(images, cot_ref, gain_ref, dtok_ref, nx_ref, inv_ref, alive_ref, dn_ref)
    for k in (0, 1):
        drain(r1.at[k, rest[k]], v1.at[k])
        total = q[k, mine[k]].astype(F32)
        for d in rings[k]:
            total = total + r1[k, back(mine[k], d, chip[k])].astype(F32)
        t_ref[:, k] = total.astype(BF16)
    for d in near[::-1]:
        send(t_ref.at[lax.rem(x + d, nx)], r2.at[x], s2.at[0], v2.at[0], x_peer(d))
    bl_ref[1] = late_wait(0)
    late_send(1)
    drain(r2.at[pl.ds(0, nx - 1)], v2.at[0])
    total = t_ref[x].astype(F32)
    for d in near:
        total = total + r2[back(x, d, nx)].astype(F32)
    u_ref[...] = total.astype(BF16)
    for k in (0, 1):
        for d in rings[1 - k][::-1]:
            send(u_ref.at[k], r3.at[k, mine[1 - k]], s3.at[k], v3.at[k], peers[1 - k](d))
        r3[k, mine[1 - k]] = u_ref[k]
    bl_ref[2] = late_wait(1)
    late_send(2)
    for k in (0, 1):
        drain(r3.at[k, rest[1 - k]], v3.at[k])
        total = r3[k, 0].astype(F32)
        for i in range(1, chip[1 - k]):
            total = total + r3[k, i].astype(F32)
        out_ref[k, c, mine[k], x] = total.astype(BF16)
        block = out_ref.at[k, c, mine[k], x]
        for d in near[::-1]:
            send(block, block, s4.at[k], v4.at[k], x_peer(d))
    bl_ref[3] = late_wait(2)
    late_send(3)
    for k in (0, 1):
        drain(out_ref.at[k, c, mine[k], pl.ds(0, nx - 1)], v4.at[k])
        block = out_ref.at[k, c, mine[k]]
        for d in rings[k]:
            send(block, block, s5.at[k], v5.at[k], peers[k](d))
    for k in (0, 1):
        drain(q.at[k, rest[k]], v5.at[k])
        send(out_ref.at[k, c], out_ref.at[k, c], s6.at[k], v6.at[k], partner)
    late_out[...] = late_wait(3)
    for k in (0, 1):
        drain(out_ref.at[k, mate], v6.at[k])
        drain(pack_ref.at[k, mate], s0.at[k])
        drain(q.at[k, rest[k]], s1.at[k])
        drain(r3.at[k, rest[1 - k]], s3.at[k])
        drain(out_ref.at[k, c, mine[k], pl.ds(0, nx - 1)], s4.at[k])
        drain(q.at[k, rest[k]], s5.at[k])
        drain(out_ref.at[k, c], s6.at[k])
    drain(r2.at[pl.ds(0, nx - 1)], s2.at[0])
    for stage, (slots, n, _, _) in enumerate(places):
        drain(slots.at[pl.ds(0, n - 1)], sl.at[stage])


def finish_kernel(dtok_ref, sum_ref, late_ref, out_ref, wi_ref, bi_ref, wo_ref, bo_ref, gain_ref, shift_ref):
    out_ref[...] = dtok_ref[...]
    one = late_ref[...].astype(F32)
    total = one * one
    for k in (0, 1):
        for i in range(55 - k):
            piece = sum_ref[k, i].astype(F32)
            total = total + piece * piece
    total = jnp.sum(jnp.sum(total, axis=1, keepdims=True), axis=0, keepdims=True)
    factor = jnp.minimum(1.0, clip_share * math.sqrt(ENTRIES) / jnp.sqrt(total + 1e-06))
    for i in range(PMAX // LINES):
        for b in range(3):
            box = (slice(i * LINES, (i + 1) * LINES), slice(b * 128, (b + 1) * 128))
            wi_ref[box] = (sum_ref[0, i * 3 + b].astype(F32) * factor).astype(BF16)
            wo_ref[box] = (sum_ref[1, i * 3 + b].astype(F32) * factor).astype(BF16)
    one = one * factor
    two = sum_ref[0, 54].astype(F32) * factor
    for b in range(6):
        at = pl.ds(b * 128, 128)
        gain_ref[at] = one[b].astype(BF16)
        shift_ref[at] = one[6 + b].astype(BF16)
    for b in range(3):
        width = min(128, PMAX - b * 128)
        bi_ref[pl.ds(b * 128, 128)] = two[b].astype(BF16)
        bo_ref[pl.ds(b * 128, width)] = two[3 + b, :width].astype(BF16)


def main(nx, ny, nz, tokens, cotangent, patch_mask, image_tiles, patches, *weights):
    w_in, b_in, w_out, ln_gain, ln_shift = weights
    args = (image_tiles.T, patches.T, tokens, cotangent, patch_mask, w_in, b_in, w_out.T, ln_gain, ln_shift)
    n, places = max(ny, nz), image_tiles.shape[0]
    shape, dma = jax.ShapeDtypeStruct, pltpu.SemaphoreType.DMA
    block = (BLOCKS // (2 * n * nx) * LINES, 128)
    sems = [(2,), (2, n), (2,), (2,), (1,), (1,), (2,), (2,), (2,), (2,), (2,), (2,), (2,), (2,)]
    return pl.pallas_call(
        lambda *refs: main_kernel(nx, ny, nz, *refs),
        name="main",
        out_shape=(shape((ROWS, C), BF16), shape((2, 2, n, nx, *block), BF16), shape((LINES, 128), BF16)),
        in_specs=[HBM] * 10,
        out_specs=(VMEM, VMEM, VMEM),
        scratch_shapes=[
            pltpu.SMEM((3, places), jnp.int32),
            pltpu.SMEM((3, places), jnp.int32),
            pltpu.VMEM((ROWS, C), BF16),
            pltpu.VMEM((ROWS, C), BF16),
            pltpu.VMEM((ROWS,), jnp.int32),
            pltpu.VMEM((PMAX, H), BF16),
            pltpu.VMEM((H,), F32),
            pltpu.VMEM((PMAX, H), BF16),
            pltpu.VMEM((C,), F32),
            pltpu.VMEM((C,), F32),
            dma((10,)),
            pltpu.VMEM((ROWS, C), F32),
            pltpu.VMEM((ROWS, 128), F32),
            pltpu.VMEM((ROWS, 128), F32),
            pltpu.VMEM((PAD_TILES, TILE, C), BF16),
            pltpu.VMEM((PAD_TILES, TILE, C), BF16),
            pltpu.VMEM((sum(SPANS) // TILE, TILE, C), BF16),
            pltpu.VMEM((3, H, C), BF16),
            pltpu.VMEM((3, H, C), BF16),
            pltpu.VMEM((PMAX, H), F32),
            pltpu.VMEM((PMAX, H), F32),
            pltpu.VMEM((H, 128), F32),
            pltpu.VMEM((LINES, 128), F32),
            pltpu.VMEM((sum(SPANS), C), BF16),
            pltpu.VMEM((sum(SPANS), C), BF16),
            pltpu.VMEM((2, H, C), F32),
            pltpu.VMEM((2, H, C), F32),
            pltpu.VMEM((H, 128), F32),
            pltpu.VMEM((2, H, PMAX), BF16),
            pltpu.VMEM((PAD_TILES, TILE, 128), F32),
            pltpu.VMEM((LINES, 128), F32),
            pltpu.VMEM((4, LINES, 128), BF16),
            pltpu.VMEM((2, LINES, 128), BF16),
            pltpu.VMEM((nz, LINES, 128), BF16),
            pltpu.VMEM((nx, LINES, 128), BF16),
            pltpu.VMEM((ny, LINES, 128), BF16),
            dma((4,)),
            dma((4,)),
            pltpu.VMEM((2, 2, n, nx, *block), BF16),
            pltpu.VMEM((2, n, nx, *block), BF16),
            pltpu.VMEM((2, n, nx, *block), BF16),
            pltpu.VMEM((2, n, nx, *block), BF16),
            pltpu.VMEM((nx, 2, *block), BF16),
            pltpu.VMEM((nx, 2, *block), BF16),
            pltpu.VMEM((2, *block), BF16),
            pltpu.VMEM((2, n, *block), BF16),
        ]
        + [dma(shape) for shape in sems],
        compiler_params=pltpu.CompilerParams(collective_id=0, has_side_effects=True, vmem_limit_bytes=24 << 20),
    )(*[pltpu.with_memory_space_constraint(v, pltpu.HBM) for v in args])


def finish(dtokens, sums, late):
    shape = jax.ShapeDtypeStruct
    shapes = ((ROWS, C), (PMAX, H), (H,), (PMAX, H), (PMAX,), (C,), (C,))
    return pl.pallas_call(
        finish_kernel,
        name="finish",
        out_shape=tuple(shape(s, BF16) for s in shapes),
        in_specs=[VMEM] * 3,
        out_specs=(VMEM,) * 7,
        compiler_params=pltpu.CompilerParams(vmem_limit_bytes=10 << 20),
    )(dtokens, sums, late)


def solution(mesh):
    ny, nz = mesh.shape["dp"] // NX, mesh.shape["group"] // 2

    def local(*args):
        dtokens, sums, late = main(NX, ny, nz, *args)
        dtokens, w_in, b_in, w_out, b_out, gain, shift = finish(
            dtokens, sums.reshape(2, BLOCKS, LINES, 128), late
        )
        return (dtokens, w_in, b_in, w_out.T, b_out, gain, shift)

    rows = P(AXES, None)
    in_specs = (rows, rows, P(AXES)) + (P(),) * 7
    out_specs = (rows,) + (P(),) * 6
    return jax.shard_map(local, mesh=mesh, in_specs=in_specs, out_specs=out_specs, check_vma=False)
```

```python
import math

import jax
import jax.numpy as jnp
from jax import lax
from jax.experimental import pallas as pl
from jax.experimental.pallas import tpu as pltpu
from jax.sharding import PartitionSpec as P

PMAX = 288
TILE = 32
TILES = 10
ROWS = TILE * TILES
C = 768
H = 384
NX = 4
SPANS = (288, 160, 96)
BASES = (0, 9, 14)
PAD_TILES = TILES + PMAX // TILE
LINES = 16
BLOCKS = 64
ENTRIES = 2 * PMAX * H + H + PMAX + 2 * C

ln_epsilon = 1e-05
clip_share = 0.5
F32 = jnp.float32
BF16 = jnp.bfloat16
MESH = pl.DeviceIdType.MESH
AXES = ("dp", "group")
VMEM = pl.BlockSpec(memory_space=pltpu.VMEM)
HBM = pl.BlockSpec(memory_space=pltpu.HBM)


def dot(a, b, da, db):
    return lax.dot_general(a, b, (((da,), (db,)), ((), ())), preferred_element_type=F32)


def gelu_pair(preact):
    scaled = preact * 0.7071067811865476
    normal_cdf = 0.5 * lax.erf(scaled) + 0.5
    density = jnp.exp2(scaled * scaled * -1.4426950408889634)
    return (preact * normal_cdf, normal_cdf + preact * 0.3989422804014327 * density)


def wide(col):
    return jnp.concatenate([col] * (C // 128), axis=1)


def column(row):
    return jnp.transpose(jnp.broadcast_to(row, (128, row.shape[1])))


def image_table(tiles_ref, patches_ref, place):
    tiles = [tiles_ref[s, place] for s in range(3)]
    counts = [patches_ref[s, place] for s in range(3)]
    starts = [jnp.int32(0), tiles[0], tiles[0] + tiles[1]]
    images = list(zip(tiles, starts, counts))
    for i, j in ((0, 1), (0, 2), (1, 2)):
        a, b = images[i], images[j]
        swap = b[0] > a[0]
        images[i] = tuple(jnp.where(swap, q, p) for p, q in zip(a, b))
        images[j] = tuple(jnp.where(swap, p, q) for p, q in zip(a, b))
    return images


def rows_of(images, t, dn_ref, alive_ref):
    source = jnp.int32(0)
    for j, (tiles, start, _) in enumerate(images):
        held = (start <= t) & (t < start + tiles)
        source = jnp.where(held, BASES[j] + t - start, source)
    return dn_ref[source].astype(F32) * wide(alive_ref[t * TILE : (t + 1) * TILE, :])


def gradients(
    loads, tiles_ref, patches_ref, tok_ref, cot_ref, mask_ref, wi_ref, bi_ref, wo_ref, gain_ref, shift_ref, pack_ref,
    nx_ref, inv_ref, alive_ref, x_ref, d_ref, dn_ref, act_ref, dpre_ref, gi_ref, go_ref, bo_ref, small_ref,
    xs_ref, ds_ref, pre_ref, dz_ref, sum_ref, wt_ref, ro_ref, late_ref,
):
    place = lax.axis_index("dp") * lax.axis_size("group") + lax.axis_index("group")
    x_ref[TILES:] = jnp.zeros((PMAX // TILE, TILE, C), BF16)
    d_ref[TILES:] = jnp.zeros((PMAX // TILE, TILE, C), BF16)
    sum_ref[...] = jnp.zeros((H, 128), F32)
    small_ref[...] = jnp.zeros((LINES, 128), F32)
    late_ref[...] = jnp.zeros((LINES, 128), F32)
    for load in loads[:6]:
        load.wait()
    images = image_table(tiles_ref, patches_ref, place)
    row = lax.broadcasted_iota(jnp.int32, (ROWS, 128), 0)
    alive = jnp.zeros((ROWS, 128), F32)
    for _, start, count in images:
        first = start * TILE
        alive = jnp.where((row >= first) & (row < first + count), 1.0, alive)
    alive_ref[...] = alive * column(mask_ref[...].astype(F32).reshape(1, ROWS))
    gain = gain_ref[...].reshape(1, C)
    shift = shift_ref[...].reshape(1, C)
    for t in range(TILES):
        rows = slice(t * TILE, (t + 1) * TILE)
        values = tok_ref[rows, :].astype(F32)
        center = values - jnp.mean(values, axis=1, keepdims=True)
        inv = lax.rsqrt(jnp.mean(center * center, axis=1, keepdims=True) + ln_epsilon)
        normal = center * inv
        nx_ref[rows, :] = normal
        inv_ref[rows, :] = jnp.broadcast_to(inv, (TILE, 128))
        x_ref[t] = ((normal * gain + shift) * wide(alive_ref[rows, :])).astype(BF16)
    for load in loads[6:]:
        load.wait()

    bias = column(bi_ref[...].reshape(1, H))
    bias = jnp.concatenate([bias, bias], axis=1)
    wt_ref[0] = jnp.transpose(wi_ref[...])
    wt_ref[1] = jnp.transpose(wo_ref[...])

    def place_rows(j, source, target):
        tiles, start, _ = images[j]
        for u in range(SPANS[j] // TILE):
            keep = jnp.where(u < tiles, 1.0, 0.0).astype(BF16)
            target[(BASES[j] + u) * TILE : (BASES[j] + u + 1) * TILE, :] = source[start + u] * keep

    def own(j):
        return slice(BASES[j] * TILE, BASES[j] * TILE + SPANS[j])

    def project_pre(j, part):
        cols = slice(part * 256, (part + 1) * 256)
        pre_ref[j % 2, :, cols] = dot(wt_ref[0, :, : SPANS[j]], xs_ref[own(j), cols], 1, 0)

    def project_dz(j, part):
        cols = slice(part * 256, (part + 1) * 256)
        dz_ref[j % 2, :, cols] = dot(wt_ref[1, :, : SPANS[j]], ds_ref[own(j), cols], 1, 0)

    def activate(j, part):
        cols = slice(part * 256, (part + 1) * 256)
        act, slope = gelu_pair(pre_ref[j % 2, :, cols] + bias)
        act_ref[j, :, cols] = act.astype(BF16)
        dpre = dz_ref[j % 2, :, cols] * slope
        dpre_ref[j, :, cols] = dpre.astype(BF16)
        sum_ref[...] += dpre[:, :128] + dpre[:, 128:]

    def reduce(j, part):
        span = SPANS[j]
        if part == 0:
            gi = dot(xs_ref[own(j), :], dpre_ref[j], 1, 1)
            gi_ref[:span, :] = gi if j == 0 else gi_ref[:span, :] + gi
        elif part == 1:
            go = dot(ds_ref[own(j), :], act_ref[j], 1, 1)
            go_ref[:span, :] = go if j == 0 else go_ref[:span, :] + go

    for j in range(3):
        place_rows(j, x_ref, xs_ref)
    for part in range(3):
        project_pre(0, part)
    for t in range(TILES):
        rows = slice(t * TILE, (t + 1) * TILE)
        d_ref[t] = (cot_ref[rows, :].astype(F32) * wide(alive_ref[rows, :])).astype(BF16)
    for j in range(3):
        place_rows(j, d_ref, ds_ref)
    for step in range(5):
        for part in range(3):
            if 0 < step < 3:
                project_pre(step, part)
            if step < 3:
                project_dz(step, part)
            if 1 <= step < 4:
                activate(step - 1, part)
            if step >= 2:
                reduce(step - 2, part)

    for b in range(3):
        small_ref[b : b + 1, :] = jnp.sum(jnp.transpose(sum_ref[b * 128 : (b + 1) * 128, :]), axis=0, keepdims=True)
    n, nx, lines = pack_ref.shape[2:5]
    each = lines // LINES

    def put(k, i, value):
        shard, at = i // each, i % each * LINES
        pack_ref[k, shard // (n * nx), shard // nx % n, shard % nx, at : at + LINES] = value

    for i in range(PMAX // LINES):
        for b in range(3):
            box = (slice(i * LINES, (i + 1) * LINES), slice(b * 128, (b + 1) * 128))
            put(0, i * 3 + b, gi_ref[box].astype(BF16))
            put(1, i * 3 + b, go_ref[box].astype(BF16))
    put(0, 54, small_ref[...].astype(BF16))
    for k, used in ((0, 55), (1, 54)):
        for i in range(used, BLOCKS):
            put(k, i, jnp.zeros((LINES, 128), BF16))
    return images


def late_sums(images, wi_ref, dpre_ref, dn_ref, nx_ref, alive_ref, late_ref, bl_ref, d_ref, ro_ref, bo_ref):
    ro_ref[TILES:] = jnp.zeros((PMAX // TILE, TILE, 128), F32)
    bo_ref[...] = jnp.zeros((H, 128), F32)
    for t in range(TILES):
        ro_ref[t] = jnp.broadcast_to(jnp.sum(d_ref[t].astype(F32), axis=1, keepdims=True), (TILE, 128))
    for j, (tiles, start, _) in enumerate(images):
        for u in range(SPANS[j] // TILE):
            bo_ref[u * TILE : (u + 1) * TILE, :] += ro_ref[start + u] * jnp.where(u < tiles, 1.0, 0.0)
    for b in range(3):
        late_ref[12 + b : 13 + b, :] = jnp.transpose(bo_ref[b * 128 : (b + 1) * 128, :])[0:1]
    for j in range(3):
        back_rows = dot(wi_ref[: SPANS[j], :], dpre_ref[j], 1, 0).astype(BF16)
        for u in range(SPANS[j] // TILE):
            dn_ref[BASES[j] + u] = back_rows[u * TILE : (u + 1) * TILE]
    gain_sum = jnp.zeros((8, C), F32)
    shift_sum = jnp.zeros((8, C), F32)
    for t in range(TILES):
        d_rows = rows_of(images, t, dn_ref, alive_ref)
        weighted = d_rows * nx_ref[t * TILE : (t + 1) * TILE, :]
        for i in range(0, TILE, 8):
            gain_sum = gain_sum + weighted[i : i + 8]
            shift_sum = shift_sum + d_rows[i : i + 8]

    gain_row = jnp.sum(gain_sum, axis=0, keepdims=True)
    shift_row = jnp.sum(shift_sum, axis=0, keepdims=True)
    for b in range(6):
        late_ref[b : b + 1, :] = gain_row[:, b * 128 : (b + 1) * 128]
        late_ref[6 + b : 7 + b, :] = shift_row[:, b * 128 : (b + 1) * 128]
    bl_ref[...] = late_ref[...].astype(BF16)


def token_gradient(images, cot_ref, gain_ref, dtok_ref, nx_ref, inv_ref, alive_ref, dn_ref):
    gain = gain_ref[...].reshape(1, C)
    for t in range(TILES):
        rows = slice(t * TILE, (t + 1) * TILE)
        normal = nx_ref[rows, :]
        scaled = rows_of(images, t, dn_ref, alive_ref) * gain
        inner = jnp.mean(scaled * normal, axis=1, keepdims=True)
        d_norm = (scaled - jnp.mean(scaled, axis=1, keepdims=True) - normal * inner) * wide(inv_ref[rows, :])
        dtok_ref[rows, :] = (cot_ref[rows, :].astype(F32) + d_norm).astype(BF16)


def ring_order(n):
    order = []
    for d in range(1, n // 2 + 1):
        order.append(d)
        if n - d != d:
            order.append(n - d)
    return order


def main_kernel(
    nx, ny, nz,
    tiles_in, patches_in, tok_in, cot_in, mask_in, wi_in, bi_in, wo_in, gain_in, shift_in,
    dtok_ref, out_ref, late_out,
    tiles_ref, patches_ref, tok_ref, cot_ref, mask_ref, wi_ref, bi_ref, wo_ref, gain_ref, shift_ref, in_sem,
    nx_ref, inv_ref, alive_ref, x_ref, d_ref, dn_ref, act_ref, dpre_ref, gi_ref, go_ref, bo_ref, small_ref,
    xs_ref, ds_ref, pre_ref, dz_ref, sum_ref, wt_ref, ro_ref, late_ref,
    bl_ref, lc, lz, lx, ly, sl, vl,
    pack_ref, r0, q, r1, t_ref, r2, u_ref, r3,
    s0, v0, s1, v1, s2, v2, s3, v3, s4, v4, s5, v5, s6, v6,
):
    pairs = (
        (tok_in, tok_ref), (mask_in, mask_ref), (gain_in, gain_ref), (shift_in, shift_ref), (tiles_in, tiles_ref),
        (patches_in, patches_ref), (cot_in, cot_ref), (wi_in, wi_ref), (wo_in, wo_ref), (bi_in, bi_ref),
    )
    loads = [pltpu.make_async_copy(a, b, in_sem.at[i]) for i, (a, b) in enumerate(pairs)]
    for load in loads:
        load.start()
    dp = lax.axis_index("dp")
    group = lax.axis_index("group")
    y, x = dp // nx, lax.rem(dp, nx)
    z, c = group // 2, lax.rem(group, 2)
    mate = 1 - c
    chip = (nz, ny)
    mine = (z, y)
    partner = (dp, z * 2 + mate)

    def z_peer(d):
        return (dp, lax.rem(z + d, nz) * 2 + c)

    def y_peer(d):
        return (lax.rem(y + d, ny) * nx + x, group)

    def x_peer(d):
        return (y * nx + lax.rem(x + d, nx), group)

    peers = (z_peer, y_peer)
    barrier = pltpu.get_barrier_semaphore()
    everyone = [partner]
    everyone += [z_peer(d) for d in range(1, nz)]
    everyone += [y_peer(d) for d in range(1, ny)]
    everyone += [x_peer(d) for d in range(1, nx)]
    for device in everyone:
        pl.semaphore_signal(barrier, inc=1, device_id=device, device_id_type=MESH)
    images = gradients(
        loads, tiles_ref, patches_ref, tok_ref, cot_ref, mask_ref, wi_ref, bi_ref, wo_ref, gain_ref, shift_ref, pack_ref,
        nx_ref, inv_ref, alive_ref, x_ref, d_ref, dn_ref, act_ref, dpre_ref, gi_ref, go_ref, bo_ref, small_ref,
        xs_ref, ds_ref, pre_ref, dz_ref, sum_ref, wt_ref, ro_ref, late_ref,
    )
    pl.semaphore_wait(barrier, len(everyone))
    def send(source, target, send_sem, recv_sem, device):
        copy = pltpu.make_async_remote_copy(
            src_ref=source, dst_ref=target, send_sem=send_sem, recv_sem=recv_sem, device_id=device, device_id_type=MESH
        )
        copy.start()
        return copy

    def drain(ref, sem):
        pltpu.make_async_copy(ref, ref, sem).wait()

    def back(at, d, n):
        return lax.rem(at - d + n, n)

    places = ((lc, 2, c, lambda d: partner), (lz, nz, z, z_peer), (lx, nx, x, x_peer), (ly, ny, y, y_peer))

    def late_send(stage):
        slots, n, at, peer = places[stage]
        for d in reversed(ring_order(n)):
            send(bl_ref.at[stage], slots.at[at], sl.at[stage], vl.at[stage], peer(d))
        slots[at] = bl_ref[stage]

    def late_wait(stage):
        slots, n, _, _ = places[stage]
        drain(slots.at[pl.ds(0, n - 1)], vl.at[stage])
        total = slots[0].astype(F32)
        for i in range(1, n):
            total = total + slots[i].astype(F32)
        return total.astype(BF16)

    near = ring_order(nx)
    rings = [ring_order(m) for m in chip]
    rest = [pl.ds(0, m - 1) for m in chip]
    orders = [ring[::-1] + [0] for ring in rings]
    steps = [(k, orders[k][i]) for i in range(max(chip)) for k in (0, 1) if i < chip[k]]
    first = {}
    for k, d in steps:
        at = lax.rem(mine[k] + d, chip[k])
        first[k, d] = send(pack_ref.at[k, mate, at], r0.at[k, at], s0.at[k], v0.at[k, d], partner)
    for k, d in steps:
        at = lax.rem(mine[k] + d, chip[k])
        first[k, d].wait_recv()
        q[k, at] = (pack_ref[k, c, at].astype(F32) + r0[k, at].astype(F32)).astype(BF16)
        if d:
            send(q.at[k, at], r1.at[k, mine[k]], s1.at[k], v1.at[k], peers[k](d))
    late_sums(images, wi_ref, dpre_ref, dn_ref, nx_ref, alive_ref, late_ref, bl_ref.at[0], d_ref, ro_ref, bo_ref)
    late_send(0)
    token_gradient(images, cot_ref, gain_ref, dtok_ref, nx_ref, inv_ref, alive_ref, dn_ref)
    for k in (0, 1):
        drain(r1.at[k, rest[k]], v1.at[k])
        total = q[k, mine[k]].astype(F32)
        for d in rings[k]:
            total = total + r1[k, back(mine[k], d, chip[k])].astype(F32)
        t_ref[:, k] = total.astype(BF16)
    for d in near[::-1]:
        send(t_ref.at[lax.rem(x + d, nx)], r2.at[x], s2.at[0], v2.at[0], x_peer(d))
    bl_ref[1] = late_wait(0)
    late_send(1)
    drain(r2.at[pl.ds(0, nx - 1)], v2.at[0])
    total = t_ref[x].astype(F32)
    for d in near:
        total = total + r2[back(x, d, nx)].astype(F32)
    u_ref[...] = total.astype(BF16)
    for k in (0, 1):
        for d in rings[1 - k][::-1]:
            send(u_ref.at[k], r3.at[k, mine[1 - k]], s3.at[k], v3.at[k], peers[1 - k](d))
        r3[k, mine[1 - k]] = u_ref[k]
    bl_ref[2] = late_wait(1)
    late_send(2)
    for k in (0, 1):
        drain(r3.at[k, rest[1 - k]], v3.at[k])
        total = r3[k, 0].astype(F32)
        for i in range(1, chip[1 - k]):
            total = total + r3[k, i].astype(F32)
        out_ref[k, c, mine[k], x] = total.astype(BF16)
        block = out_ref.at[k, c, mine[k], x]
        for d in near[::-1]:
            send(block, block, s4.at[k], v4.at[k], x_peer(d))
    bl_ref[3] = late_wait(2)
    late_send(3)
    for k in (0, 1):
        drain(out_ref.at[k, c, mine[k], pl.ds(0, nx - 1)], v4.at[k])
        block = out_ref.at[k, c, mine[k]]
        for d in rings[k][::-1]:
            send(block, block, s5.at[k], v5.at[k], peers[k](d))
    for k in (0, 1):
        drain(q.at[k, rest[k]], v5.at[k])
        send(out_ref.at[k, c], out_ref.at[k, c], s6.at[k], v6.at[k], partner)
    late_out[...] = late_wait(3)
    for k in (0, 1):
        drain(out_ref.at[k, mate], v6.at[k])
        drain(pack_ref.at[k, mate], s0.at[k])
        drain(q.at[k, rest[k]], s1.at[k])
        drain(r3.at[k, rest[1 - k]], s3.at[k])
        drain(out_ref.at[k, c, mine[k], pl.ds(0, nx - 1)], s4.at[k])
        drain(q.at[k, rest[k]], s5.at[k])
        drain(out_ref.at[k, c], s6.at[k])
    drain(r2.at[pl.ds(0, nx - 1)], s2.at[0])
    for stage, (slots, n, _, _) in enumerate(places):
        drain(slots.at[pl.ds(0, n - 1)], sl.at[stage])


def finish_kernel(dtok_ref, sum_ref, late_ref, out_ref, wi_ref, bi_ref, wo_ref, bo_ref, gain_ref, shift_ref):
    out_ref[...] = dtok_ref[...]
    one = late_ref[...].astype(F32)
    total = one * one
    for k in (0, 1):
        for i in range(55 - k):
            piece = sum_ref[k, i].astype(F32)
            total = total + piece * piece
    total = jnp.sum(jnp.sum(total, axis=1, keepdims=True), axis=0, keepdims=True)
    factor = jnp.minimum(1.0, clip_share * math.sqrt(ENTRIES) / jnp.sqrt(total + 1e-06))
    for i in range(PMAX // LINES):
        for b in range(3):
            box = (slice(i * LINES, (i + 1) * LINES), slice(b * 128, (b + 1) * 128))
            wi_ref[box] = (sum_ref[0, i * 3 + b].astype(F32) * factor).astype(BF16)
            wo_ref[box] = (sum_ref[1, i * 3 + b].astype(F32) * factor).astype(BF16)
    one = one * factor
    two = sum_ref[0, 54].astype(F32) * factor
    for b in range(6):
        at = pl.ds(b * 128, 128)
        gain_ref[at] = one[b].astype(BF16)
        shift_ref[at] = one[6 + b].astype(BF16)
    for b in range(3):
        width = min(128, PMAX - b * 128)
        bi_ref[pl.ds(b * 128, 128)] = two[b].astype(BF16)
        bo_ref[pl.ds(b * 128, width)] = one[12 + b, :width].astype(BF16)


def main(nx, ny, nz, tokens, cotangent, patch_mask, image_tiles, patches, *weights):
    w_in, b_in, w_out, ln_gain, ln_shift = weights
    args = (image_tiles.T, patches.T, tokens, cotangent, patch_mask, w_in, b_in, w_out.T, ln_gain, ln_shift)
    n, places = max(ny, nz), image_tiles.shape[0]
    shape, dma = jax.ShapeDtypeStruct, pltpu.SemaphoreType.DMA
    block = (BLOCKS // (2 * n * nx) * LINES, 128)
    sems = [(2,), (2, n), (2,), (2,), (1,), (1,), (2,), (2,), (2,), (2,), (2,), (2,), (2,), (2,)]
    return pl.pallas_call(
        lambda *refs: main_kernel(nx, ny, nz, *refs),
        name="main",
        out_shape=(shape((ROWS, C), BF16), shape((2, 2, n, nx, *block), BF16), shape((LINES, 128), BF16)),
        in_specs=[HBM] * 10,
        out_specs=(VMEM, VMEM, VMEM),
        scratch_shapes=[
            pltpu.SMEM((3, places), jnp.int32),
            pltpu.SMEM((3, places), jnp.int32),
            pltpu.VMEM((ROWS, C), BF16),
            pltpu.VMEM((ROWS, C), BF16),
            pltpu.VMEM((ROWS,), jnp.int32),
            pltpu.VMEM((PMAX, H), BF16),
            pltpu.VMEM((H,), F32),
            pltpu.VMEM((PMAX, H), BF16),
            pltpu.VMEM((C,), F32),
            pltpu.VMEM((C,), F32),
            dma((10,)),
            pltpu.VMEM((ROWS, C), F32),
            pltpu.VMEM((ROWS, 128), F32),
            pltpu.VMEM((ROWS, 128), F32),
            pltpu.VMEM((PAD_TILES, TILE, C), BF16),
            pltpu.VMEM((PAD_TILES, TILE, C), BF16),
            pltpu.VMEM((sum(SPANS) // TILE, TILE, C), BF16),
            pltpu.VMEM((3, H, C), BF16),
            pltpu.VMEM((3, H, C), BF16),
            pltpu.VMEM((PMAX, H), F32),
            pltpu.VMEM((PMAX, H), F32),
            pltpu.VMEM((H, 128), F32),
            pltpu.VMEM((LINES, 128), F32),
            pltpu.VMEM((sum(SPANS), C), BF16),
            pltpu.VMEM((sum(SPANS), C), BF16),
            pltpu.VMEM((2, H, C), F32),
            pltpu.VMEM((2, H, C), F32),
            pltpu.VMEM((H, 128), F32),
            pltpu.VMEM((2, H, PMAX), BF16),
            pltpu.VMEM((PAD_TILES, TILE, 128), F32),
            pltpu.VMEM((LINES, 128), F32),
            pltpu.VMEM((4, LINES, 128), BF16),
            pltpu.VMEM((2, LINES, 128), BF16),
            pltpu.VMEM((nz, LINES, 128), BF16),
            pltpu.VMEM((nx, LINES, 128), BF16),
            pltpu.VMEM((ny, LINES, 128), BF16),
            dma((4,)),
            dma((4,)),
            pltpu.VMEM((2, 2, n, nx, *block), BF16),
            pltpu.VMEM((2, n, nx, *block), BF16),
            pltpu.VMEM((2, n, nx, *block), BF16),
            pltpu.VMEM((2, n, nx, *block), BF16),
            pltpu.VMEM((nx, 2, *block), BF16),
            pltpu.VMEM((nx, 2, *block), BF16),
            pltpu.VMEM((2, *block), BF16),
            pltpu.VMEM((2, n, *block), BF16),
        ]
        + [dma(shape) for shape in sems],
        compiler_params=pltpu.CompilerParams(collective_id=0, has_side_effects=True, vmem_limit_bytes=24 << 20),
    )(*[pltpu.with_memory_space_constraint(v, pltpu.HBM) for v in args])


def finish(dtokens, sums, late):
    shape = jax.ShapeDtypeStruct
    shapes = ((ROWS, C), (PMAX, H), (H,), (PMAX, H), (PMAX,), (C,), (C,))
    return pl.pallas_call(
        finish_kernel,
        name="finish",
        out_shape=tuple(shape(s, BF16) for s in shapes),
        in_specs=[VMEM] * 3,
        out_specs=(VMEM,) * 7,
        compiler_params=pltpu.CompilerParams(vmem_limit_bytes=10 << 20),
    )(dtokens, sums, late)


def solution(mesh):
    ny, nz = mesh.shape["dp"] // NX, mesh.shape["group"] // 2

    def local(*args):
        dtokens, sums, late = main(NX, ny, nz, *args)
        dtokens, w_in, b_in, w_out, b_out, gain, shift = finish(
            dtokens, sums.reshape(2, BLOCKS, LINES, 128), late
        )
        return (dtokens, w_in, b_in, w_out.T, b_out, gain, shift)

    rows = P(AXES, None)
    in_specs = (rows, rows, P(AXES)) + (P(),) * 7
    out_specs = (rows,) + (P(),) * 6
    return jax.shard_map(local, mesh=mesh, in_specs=in_specs, out_specs=out_specs, check_vma=False)
```
